32 devices in a mesh: seq: 8 (over z, x), tp: 4 (over y, core).
Axes of the slice: x: 2, y: 2, z: 4, core: 2. Of those that a mesh axis runs over, the one named last changes fastest.
Arguments:
- inputs: bfloat16 [1024, 2560], P(('seq', 'tp')), may hold values from -6 to 6
- cotangent: bfloat16 [1024, 2560], P('seq'), may hold values from -6 to 6
- vectors: float32 [18, 2560], replicated, may hold values from -10 to 1.5
- mixing_projection_weight: bfloat16 [3, 2560, 2560], P(None, 'seq', 'tp'), may hold values from -0.125 to 0.125
- output_projection_weight: bfloat16 [2560, 2560], P('tp', 'seq'), may hold values from -0.125 to 0.125
- low_rank_down_weight: bfloat16 [2560, 512], P(('seq', 'tp')), may hold values from -0.125 to 0.125
- low_rank_up_weight: bfloat16 [512, 2560], P('seq', 'tp'), may hold values from -0.625 to 0.625
- channel_key_matrix: bfloat16 [2560, 10240], P('seq', 'tp'), may hold values from -0.125 to 0.125
- channel_value_matrix: bfloat16 [10240, 2560], P('tp', 'seq'), may hold values from -0.0625 to 0.0625
Outputs:
- output: bfloat16 [1024, 2560], P(('seq', 'tp'))
- grad_inputs: float32 [1024, 2560], P(('seq', 'tp'))
- grad_vectors: float32 [18, 2560], P(None, ('seq', 'tp'))
- grad_mix_proj: float32 [3, 2560, 2560], P(None, 'seq', 'tp')
- grad_out_proj: float32 [2560, 2560], P('tp', 'seq')
- grad_lora_down: float32 [2560, 512], P(('seq', 'tp'))
- grad_lora_up: float32 [512, 2560], P('seq', 'tp')
- grad_ffn_key: float32 [2560, 10240], P('seq', 'tp')
- grad_ffn_value: float32 [10240, 2560], P('tp', 'seq')
The draws below stay inside these ranges and needn't reach their ends.
All inputs are finite; a program needn't handle non-finite values.
Results may differ from the reference program's by a relative error of at most 0.03.
Values may be sent and summed in bfloat16 or wider, within the bound.
No kernel may reach another device: no remote copies, remote signals or barrier semaphores. Data moves between devices by JAX's collectives and lax.ppermute only.
A program may use at most 256 MiB of HBM per device.

```python
import math
import jax
import jax.numpy as jnp
from jax import lax

MODEL_WIDTH = 2560
HEAD = 64
FF = 10240
DECAY_RANK = 96
RATE_RANK = 96
LOW_RANK_TOTAL = 512
TOKENS = 1024


def draw_vectors(key, part):
    lows = [0.6, -0.3, 0.6, -0.3, 0.0, 0.0, 0.0, 0.0, 0.0, 0.0, -9.0, -5.0, 0.5, 0.0, -1.0, 0.5, -0.3, 0.0]
    highs = [1.4, 0.3, 1.4, 0.3, 1.0, 1.0, 1.0, 1.0, 1.0, 1.0, -2.0, 0.0, 1.5, 1.0, 1.0, 1.5, 0.3, 1.0]
    bottom = jnp.array(lows, jnp.float32)
    top = jnp.array(highs, jnp.float32)
    base = jax.random.uniform(key, (18, MODEL_WIDTH), jnp.float32)
    return bottom[:, None] + (top - bottom)[:, None] * base


def level_of(rng, shape, shards, smallest, largest):
    factor_of, own = 1.0, jax.random.fold_in(rng, 6)
    for position, blocks in shards:
        draws = jnp.exp(jax.random.uniform(jax.random.fold_in(own, position), (blocks,), jnp.float32, smallest / len(shards), largest / len(shards)))
        factor_of = factor_of * jnp.repeat(draws, shape[position] // blocks).reshape([-1 if axis == position else 1 for axis in range(len(shape))])
    return factor_of


def scatter_about(rng, shape, scale, limit, cuts=(), dtype=jnp.bfloat16):
    loudness = level_of(rng, shape, cuts, -0.22, 0.18) if cuts else 1.0
    result = jax.random.normal(rng, shape, jnp.float32) * scale * loudness
    return jnp.minimum(jnp.maximum(result, -limit), limit).astype(dtype)


def setup_inputs(seed: int = 0) -> dict:
    key_of = jax.random.split(jax.random.key(seed), 10)
    return {
        "inputs": scatter_about(key_of[0], (TOKENS, MODEL_WIDTH), 1.0, 6.0, ((0, 32),)),
        "cotangent": scatter_about(key_of[1], (TOKENS, MODEL_WIDTH), 1.0, 6.0, ((0, 8),)),
        "vectors": draw_vectors(jax.random.fold_in(key_of[9], 71), 0),
        "mixing_projection_weight": scatter_about(key_of[3], (3, MODEL_WIDTH, MODEL_WIDTH), MODEL_WIDTH ** -0.5, 0.125, ((1, 8), (2, 4))),
        "output_projection_weight": scatter_about(key_of[4], (MODEL_WIDTH, MODEL_WIDTH), MODEL_WIDTH ** -0.5, 0.125, ((0, 4), (1, 8))),
        "low_rank_down_weight": scatter_about(key_of[5], (MODEL_WIDTH, LOW_RANK_TOTAL), MODEL_WIDTH ** -0.5, 0.125, ((0, 32),)),
        "low_rank_up_weight": scatter_about(key_of[6], (LOW_RANK_TOTAL, MODEL_WIDTH), DECAY_RANK ** -0.5, 0.625, ((0, 8), (1, 4))),
        "channel_key_matrix": scatter_about(key_of[7], (MODEL_WIDTH, FF), MODEL_WIDTH ** -0.5, 0.125, ((0, 8), (1, 4))),
        "channel_value_matrix": scatter_about(key_of[8], (FF, MODEL_WIDTH), FF ** -0.5, 0.0625, ((0, 4), (1, 8))),
    }


EPS_LN = 1e-05
EPS_GN = 0.00064
EPS_KEY = 1e-06
DECAY_SCALE = 0.606531
HIGHEST = lax.Precision.HIGHEST

def product_term(left, right):
    return jnp.dot(left, right, preferred_element_type=jnp.float32)

def across(left, right):
    return lax.dot_general(left, right, (((0,), (0,)), ((), ())), preferred_element_type=jnp.float32)

def versus_term(left, right):
    return lax.dot_general(left, right, (((1,), (1,)), ((), ())), preferred_element_type=jnp.float32)

def layer_norm(value, gain, bias):
    center = value - lax.optimization_barrier(jnp.mean(value, -1, keepdims=True))
    spread = lax.optimization_barrier(jnp.mean(center * center, -1, keepdims=True))
    return center * lax.rsqrt(spread + EPS_LN) * gain + bias

def norm_back(value, gain, grad):
    center = value - lax.optimization_barrier(jnp.mean(value, -1, keepdims=True))
    scale = lax.rsqrt(lax.optimization_barrier(jnp.mean(center * center, -1, keepdims=True)) + EPS_LN)
    unit = center * scale
    weighted = grad * gain
    residual_sum_result = scale * (weighted - lax.optimization_barrier(jnp.mean(weighted, -1, keepdims=True)) - unit * lax.optimization_barrier(jnp.mean(weighted * unit, -1, keepdims=True)))
    return (residual_sum_result, lax.optimization_barrier(jnp.sum(grad * unit, 0)), lax.optimization_barrier(jnp.sum(grad, 0)))

def prepare(keys, decay_preactivation, rate_preactivation, key_scale, key_mix):
    width = keys.shape[1]
    array_shape = (keys.shape[0], width // HEAD, HEAD)
    decay = jnp.exp(-DECAY_SCALE * jax.nn.sigmoid(decay_preactivation)).reshape(array_shape)
    rate = jax.nn.sigmoid(rate_preactivation)
    scaled = (keys * key_scale).reshape(array_shape)
    direction = scaled * lax.rsqrt(lax.optimization_barrier(jnp.sum(scaled * scaled, -1, keepdims=True)) + EPS_KEY)
    adjusted_lookup_vectors = (keys * (1.0 + (rate - 1.0) * key_mix)).reshape(array_shape)
    removal = direction * rate.reshape(array_shape)
    return (decay, direction, removal, adjusted_lookup_vectors)

def final_update_phase(blended_signal, acceptance_vectors, adjusted_lookup_vectors, payload_vectors, sigmoid_valve_signal, standardize_gain, standardize_offset, extra_credit_coefficient):
    width = standardize_gain.shape[0]
    pairwise_dot_sum = (width // HEAD, HEAD)
    center = blended_signal - lax.optimization_barrier(jnp.mean(blended_signal, -1, keepdims=True))
    spread = lax.optimization_barrier(jnp.mean(center * center, -1, keepdims=True))
    standardized_signal = center * lax.rsqrt(spread + EPS_GN) * standardize_gain.reshape(pairwise_dot_sum) + standardize_offset.reshape(pairwise_dot_sum)
    extra_credit_addend = lax.optimization_barrier(jnp.sum(acceptance_vectors * adjusted_lookup_vectors * extra_credit_coefficient.reshape(pairwise_dot_sum), -1, keepdims=True)) * payload_vectors
    residual_sum_result = (standardized_signal + extra_credit_addend) * sigmoid_valve_signal.reshape(sigmoid_valve_signal.shape[0], pairwise_dot_sum[0], pairwise_dot_sum[1])
    return residual_sum_result.reshape(blended_signal.shape[0], width)

def recur(decay, direction, removal, payload_vectors, adjusted_lookup_vectors, acceptance_vectors):
    count, heads, size = decay.shape
    block = math.gcd(count, 256)

    def step(state, item):
        dec, unit, rem, val, key_in, rec = item
        along = jnp.einsum('hvk,hk->hv', state, unit, precision=HIGHEST)
        state = state * dec[:, None, :] - along[:, :, None] * rem[:, None, :] + val[:, :, None] * key_in[:, None, :]
        return (state, jnp.einsum('hvk,hk->hv', state, rec, precision=HIGHEST))

    def run_block(state, items):
        return lax.scan(step, state, items)
    run_block = jax.checkpoint(run_block)
    items = tuple((a.reshape(count // block, block, heads, size) for a in (decay, direction, removal, payload_vectors, adjusted_lookup_vectors, acceptance_vectors)))
    start = jnp.zeros((heads, size, size), jnp.float32)
    final, outs = lax.scan(run_block, start, items)
    return outs.reshape(count, heads, size)

def middle_map(acceptance_vectors, keys, payload_vectors, decay_preactivation, rate_preactivation, sigmoid_valve_signal, params):
    array_shape = (keys.shape[0], keys.shape[1] // HEAD, HEAD)
    decay, direction, removal, adjusted_lookup_vectors = prepare(keys, decay_preactivation, rate_preactivation, params[0], params[1])
    rec3 = acceptance_vectors.reshape(array_shape)
    val3 = payload_vectors.reshape(array_shape)
    blended_signal = recur(decay, direction, removal, val3, adjusted_lookup_vectors, rec3)
    return final_update_phase(blended_signal, rec3, adjusted_lookup_vectors, val3, sigmoid_valve_signal, params[3], params[4], params[2])

def reference(inputs, cotangent, vectors, mixing_projection_weight, output_projection_weight, low_rank_down_weight, low_rank_up_weight, channel_key_matrix, channel_value_matrix):
    bfloat_cast = jnp.bfloat16
    fl = jnp.float32
    width = inputs.shape[1]
    resid = inputs.astype(fl)
    normed1 = layer_norm(resid, vectors[0], vectors[1]).astype(bfloat_cast)
    first = normed1.astype(fl)
    delta1 = jnp.concatenate([jnp.zeros((1, width), fl), first[:-1]], 0) - first
    mixing_factors = [(first + delta1 * vectors[4 + index]).astype(bfloat_cast) for index in range(6)]
    acceptance_vectors = product_term(mixing_factors[0], mixing_projection_weight[0])
    keys = product_term(mixing_factors[2], mixing_projection_weight[1])
    payload_vectors = product_term(mixing_factors[3], mixing_projection_weight[2])
    decay_hyperbolic = jnp.tanh(product_term(mixing_factors[1], low_rank_down_weight[:, :DECAY_RANK]))
    decay_hidden_rows = decay_hyperbolic.astype(bfloat_cast)
    decay_preactivation = vectors[10] + product_term(decay_hidden_rows, low_rank_up_weight[:DECAY_RANK])
    rate_hidden_rows = product_term(mixing_factors[4], low_rank_down_weight[:, DECAY_RANK:DECAY_RANK + RATE_RANK]).astype(bfloat_cast)
    rate_preactivation = vectors[11] + product_term(rate_hidden_rows, low_rank_up_weight[DECAY_RANK:DECAY_RANK + RATE_RANK])
    gate_logistic = jax.nn.sigmoid(product_term(mixing_factors[5], low_rank_down_weight[:, DECAY_RANK + RATE_RANK:]))
    gate_hidden_rows = gate_logistic.astype(bfloat_cast)
    sigmoid_valve_signal = product_term(gate_hidden_rows, low_rank_up_weight[DECAY_RANK + RATE_RANK:])
    mixer, middle_back = jax.vjp(middle_map, acceptance_vectors, keys, payload_vectors, decay_preactivation, rate_preactivation, sigmoid_valve_signal, vectors[12:17])
    mixer_b = mixer.astype(bfloat_cast)
    middle = resid + product_term(mixer_b, output_projection_weight)
    normed2 = layer_norm(middle, vectors[2], vectors[3]).astype(bfloat_cast)
    second = normed2.astype(fl)
    delta2 = jnp.concatenate([jnp.zeros((1, width), fl), second[:-1]], 0) - second
    ffn_in = (second + delta2 * vectors[17]).astype(bfloat_cast)
    ffn_pre = product_term(ffn_in, channel_key_matrix)
    active = jax.nn.relu(ffn_pre)
    hidden = (active * active).astype(bfloat_cast)
    output = (middle + product_term(hidden, channel_value_matrix)).astype(bfloat_cast)
    grad_value = across(hidden, cotangent)
    grad_hidden = versus_term(cotangent, channel_value_matrix)
    grad_pre = (grad_hidden * 2.0 * active).astype(bfloat_cast)
    grad_key = across(ffn_in, grad_pre)
    grad_ffn = versus_term(grad_pre, channel_key_matrix)
    carried2 = grad_ffn * vectors[17]
    grad_normed2 = grad_ffn * (1.0 - vectors[17]) + jnp.concatenate([carried2[1:], jnp.zeros((1, width), fl)], 0)
    grad_mu_ffn = lax.optimization_barrier(jnp.sum(grad_ffn * delta2, 0))
    norm_part, gain2_grad, bias2_grad = norm_back(middle, vectors[2], grad_normed2)
    grad_middle = cotangent.astype(fl) + norm_part
    grad_middle_b = grad_middle.astype(bfloat_cast)
    grad_out = across(mixer_b, grad_middle_b)
    grad_mixer = versus_term(grad_middle_b, output_projection_weight)
    back = middle_back(grad_mixer)
    receptance_gradient = back[0].astype(bfloat_cast)
    key_gradient = back[1].astype(bfloat_cast)
    value_gradient = back[2].astype(bfloat_cast)
    decay_gradient = back[3].astype(bfloat_cast)
    rate_gradient = back[4].astype(bfloat_cast)
    gate_gradient = back[5].astype(bfloat_cast)
    param_grad = back[6]
    grad_mix = jnp.stack([across(mixing_factors[0], receptance_gradient), across(mixing_factors[2], key_gradient), across(mixing_factors[3], value_gradient)])
    decay_inner_rows = (versus_term(decay_gradient, low_rank_up_weight[:DECAY_RANK]) * (1.0 - decay_hyperbolic * decay_hyperbolic)).astype(bfloat_cast)
    rate_inner_rows = versus_term(rate_gradient, low_rank_up_weight[DECAY_RANK:DECAY_RANK + RATE_RANK]).astype(bfloat_cast)
    gate_inner_rows = (versus_term(gate_gradient, low_rank_up_weight[DECAY_RANK + RATE_RANK:]) * gate_logistic * (1.0 - gate_logistic)).astype(bfloat_cast)
    grad_up = jnp.concatenate([across(decay_hidden_rows, decay_gradient), across(rate_hidden_rows, rate_gradient), across(gate_hidden_rows, gate_gradient)], 0)
    grad_down = jnp.concatenate([across(mixing_factors[1], decay_inner_rows), across(mixing_factors[4], rate_inner_rows), across(mixing_factors[5], gate_inner_rows)], 1)
    mixing_gradients = [versus_term(receptance_gradient, mixing_projection_weight[0]), versus_term(decay_inner_rows, low_rank_down_weight[:, :DECAY_RANK]), versus_term(key_gradient, mixing_projection_weight[1]), versus_term(value_gradient, mixing_projection_weight[2]), versus_term(rate_inner_rows, low_rank_down_weight[:, DECAY_RANK:DECAY_RANK + RATE_RANK]), versus_term(gate_inner_rows, low_rank_down_weight[:, DECAY_RANK + RATE_RANK:])]
    carried1 = jnp.zeros_like(resid)
    staying = jnp.zeros_like(resid)
    mu_grads = []
    for index in range(6):
        carried1 = carried1 + mixing_gradients[index] * vectors[4 + index]
        staying = staying + mixing_gradients[index] * (1.0 - vectors[4 + index])
        mu_grads.append(lax.optimization_barrier(jnp.sum(mixing_gradients[index] * delta1, 0)))
    grad_normed1 = staying + jnp.concatenate([carried1[1:], jnp.zeros((1, width), fl)], 0)
    input_part, gain1_grad, bias1_grad = norm_back(resid, vectors[0], grad_normed1)
    grad_inputs = grad_middle + input_part
    rows = [gain1_grad, bias1_grad, gain2_grad, bias2_grad] + mu_grads
    rows = rows + [lax.optimization_barrier(jnp.sum(back[3], 0)), lax.optimization_barrier(jnp.sum(back[4], 0)), param_grad[0], param_grad[1], param_grad[2], param_grad[3], param_grad[4], grad_mu_ffn]
    grad_vectors = jnp.stack(rows)
    return (output, grad_inputs, grad_vectors, grad_mix, grad_out, grad_down, grad_up, grad_key, grad_value)
```

```python
import math

import jax
import jax.numpy as jnp
from jax import lax
from jax.experimental import pallas as pl
from jax.experimental.pallas import tpu as pltpu
from jax.sharding import PartitionSpec as P

HEAD = 64
PAIR = 2 * HEAD
DECAY_RANK = 96
RATE_RANK = 96
EPS_LN = 1e-05
EPS_GN = 0.00064
EPS_KEY = 1e-06
DECAY_SCALE = 0.606531
BF = jnp.bfloat16
FL = jnp.float32
NN = (((1,), (0,)), ((), ()))
NT = (((1,), (1,)), ((), ()))
TN = (((0,), (0,)), ((), ()))


def parts(a):
    if isinstance(a, tuple):
        return a
    high = a.astype(BF)
    return high, (a - high.astype(FL)).astype(BF)


def dot(a, b, dims):
    return lax.dot_general(a, b, dims, preferred_element_type=FL)


def mm(a, b, dims=NN):
    (ah, al), (bh, bl) = parts(a), parts(b)
    return dot(ah, bh, dims) + (dot(ah, bl, dims) + dot(al, bh, dims))


def mm_ones(ones, x, dims=NN):
    first = x.astype(BF)
    rest = x - first.astype(FL)
    second = rest.astype(BF)
    third = (rest - second.astype(FL)).astype(BF)
    return dot(ones, first, dims) + (dot(ones, second, dims) + dot(ones, third, dims))


def left_lanes(shape):
    return lax.broadcasted_iota(jnp.int32, shape, len(shape) - 1) < HEAD


def head_sum(x):
    mask = left_lanes(x.shape)
    left = jnp.sum(jnp.where(mask, x, 0.0), -1, keepdims=True)
    right = jnp.sum(jnp.where(mask, 0.0, x), -1, keepdims=True)
    return jnp.where(mask, left, right)


def spread(x):
    mask = left_lanes(x.shape)
    return jnp.concatenate([jnp.where(mask, x, 0.0), jnp.where(mask, 0.0, x)], 0)


def squeeze(x):
    half = x.shape[0] // 2
    return x[:half] + x[half:]


def same_head(rows, span):
    r = lax.broadcasted_iota(jnp.int32, (rows, PAIR), 0)
    c = lax.broadcasted_iota(jnp.int32, (rows, PAIR), 1)
    return (r >= span) == (c >= HEAD)


def prepare(r, k, v, dp, rp, vec):
    sig = jax.nn.sigmoid(dp)
    logd = -DECAY_SCALE * sig
    rate = jax.nn.sigmoid(rp)
    scaled = k * vec[0:1]
    inv_norm = lax.rsqrt(head_sum(scaled * scaled) + EPS_KEY)
    unit = scaled * inv_norm
    mod = k * (1.0 + (rate - 1.0) * vec[1:2])
    return sig, logd, rate, inv_norm, unit, mod, unit * rate


def tri(n, strict, upper=False):
    r = lax.broadcasted_iota(jnp.int32, (n, n), 0)
    c = lax.broadcasted_iota(jnp.int32, (n, n), 1)
    if upper:
        r, c = c, r
    return (r > c) if strict else (r >= c)


def chunk_of(r, v, logd, unit, mod, removal):
    span = r.shape[0]
    total = mm_ones(tri(span, False).astype(FL).astype(BF), logd)
    last = total[span - 1 : span]
    c, before, inverse, ratio = (
        jnp.exp(total),
        jnp.exp(total - logd),
        jnp.exp(-total),
        jnp.exp(last - total),
    )
    out = {
        "c": c,
        "before": before,
        "inverse": inverse,
        "ratio": ratio,
        "end": jnp.exp(last),
        "ue": spread(unit * before),
        "re": spread(r * c),
        "kl": spread(mod * inverse),
        "bl": spread(removal * inverse),
        "kd": spread(mod * ratio),
        "bd": spread(removal * ratio),
        "v": spread(v),
    }
    left = parts(jnp.concatenate([out["ue"], out["re"]], 0))
    right = parts(jnp.concatenate([out["bl"], out["kl"]], 0))
    both = mm(left, right, NT)
    rows = 2 * span
    r_id = lax.broadcasted_iota(jnp.int32, (rows, rows), 0)
    c_id = lax.broadcasted_iota(jnp.int32, (rows, rows), 1)
    head = (r_id >= span) == (c_id >= span)
    strict = head & (r_id > c_id)
    inclusive = head & (r_id >= c_id)
    out["strict"], out["inclusive"] = strict, inclusive
    out["ub"] = jnp.where(strict, both[:rows, :rows], 0.0)
    out["uk"] = jnp.where(strict, both[:rows, rows:], 0.0)
    out["rb"] = jnp.where(inclusive, both[rows:, :rows], 0.0)
    out["rk"] = jnp.where(inclusive, both[rows:, rows:], 0.0)
    return out


def unit_lower_inverse(lower, span):
    rows = lower.shape[0]
    r = lax.broadcasted_iota(jnp.int32, (rows, rows), 0)
    c = lax.broadcasted_iota(jnp.int32, (rows, rows), 1)
    result = None
    size = 1
    while size < span:
        select = (r // (2 * size) == c // (2 * size)) & (r // size != c // size)
        coupling = jnp.where(select, lower, 0.0)
        if result is None:
            result = jnp.where(r == c, 1.0, 0.0) - coupling
        else:
            split = parts(result)
            result = result - mm(split, mm(coupling, split))
        size *= 2
    return result


def diagonal(row):
    r = lax.broadcasted_iota(jnp.int32, (PAIR, PAIR), 0)
    c = lax.broadcasted_iota(jnp.int32, (PAIR, PAIR), 1)
    return jnp.where(r == c, row, 0.0)


def span_of(count):
    return math.gcd(count, HEAD)


def local_kernel(r_ref, k_ref, v_ref, dp_ref, rp_ref, vec_ref, reach_ref, out_ref, state_ref, inverse_ref):
    r, k, v = r_ref[...], k_ref[...], v_ref[...]
    count = r.shape[0]
    span = span_of(count)
    vec = vec_ref[...]
    _, logd, _, _, unit, mod, removal = prepare(r, k, v, dp_ref[...], rp_ref[...], vec)
    move = add = None
    for index in range(count // span):
        at = slice(index * span, (index + 1) * span)
        q = chunk_of(r[at], v[at], logd[at], unit[at], mod[at], removal[at])
        inverse = unit_lower_inverse(q["ub"], span)
        inverse_ref[0, index] = squeeze(inverse)
        vs = parts(q["v"])
        side = mm(inverse, jnp.concatenate([q["ue"], mm(q["uk"], vs)], 1))
        side = parts(side)
        read = mm(q["rb"], side)
        reach = q["re"] - read[:, :PAIR]
        local = mm(q["rk"], vs) - read[:, PAIR:]
        gone = mm(q["bd"], side, TN)
        step_move = diagonal(q["end"]) - gone[:, :PAIR]
        step_add = mm(q["kd"], vs, TN) - gone[:, PAIR:]
        if index == 0:
            move, add = step_move, step_add
        else:
            so_far = parts(jnp.concatenate([move, add], 1))
            both = mm(reach, so_far)
            reach, local = both[:, :PAIR], local + both[:, PAIR:]
            both = mm(step_move, so_far)
            move, add = both[:, :PAIR], step_add + both[:, PAIR:]
        reach_ref[at, :] = squeeze(reach)
        out_ref[at, :] = squeeze(local)
    state_ref[0, 0] = squeeze(move).astype(BF)
    state_ref[0, 1] = squeeze(add).astype(BF)


def pair_spec(rows):
    return pl.BlockSpec((rows, PAIR), lambda p: (0, p))


def block_spec(*lead):
    return pl.BlockSpec((1, *lead), lambda p: (p,) + (0,) * len(lead))


def local_scan(r, k, v, dp, rp, vec):
    count, local = r.shape
    pairs, chunks = local // PAIR, count // span_of(count)
    span = span_of(count)
    return pl.pallas_call(
        local_kernel,
        grid=(pairs,),
        in_specs=[pair_spec(count)] * 5 + [pair_spec(8)],
        out_specs=[
            pair_spec(count),
            pair_spec(count),
            block_spec(2, HEAD, PAIR),
            block_spec(chunks, span, 2 * span),
        ],
        out_shape=[
            jax.ShapeDtypeStruct((count, local), FL),
            jax.ShapeDtypeStruct((count, local), FL),
            jax.ShapeDtypeStruct((pairs, 2, HEAD, PAIR), BF),
            jax.ShapeDtypeStruct((pairs, chunks, span, 2 * span), FL),
        ],
        name="local_scan",
    )(r, k, v, dp, rp, vec)


def group_norm(y, vec):
    center = y - head_sum(y) * (1.0 / HEAD)
    scale = lax.rsqrt(head_sum(center * center) * (1.0 / HEAD) + EPS_GN)
    return center * scale, scale


def finish_kernel(place_ref, *refs):
    others, (reach_ref, out_ref, r_ref, k_ref, v_ref, rp_ref, gate_ref, vec_ref), (
        mixer_ref,
        mixed_ref,
        enter_ref,
    ) = refs[:-11], refs[-11:-3], refs[-3:]
    place = place_ref[0]
    seen = len(others)
    for p in range(reach_ref.shape[1] // PAIR):
        lanes = slice(p * PAIR, (p + 1) * PAIR)
        state = jnp.zeros((PAIR, PAIR), FL)
        for k in range(seen, 0, -1):
            slot = others[k - 1]
            move = spread(slot[p, 0].astype(FL)).astype(BF)
            high, low = parts(state)
            new = dot(move, high, NN) + dot(move, low, NN) + spread(slot[p, 1].astype(FL))
            state = jnp.where(k <= place, new, 0.0)
        enter_ref[p] = squeeze(state)
        vec = vec_ref[:, lanes]
        r, v = r_ref[:, lanes], v_ref[:, lanes]
        y = out_ref[:, lanes] + mm(reach_ref[:, lanes], state)
        mixed_ref[:, lanes] = y
        unit, _ = group_norm(y, vec)
        rate = jax.nn.sigmoid(rp_ref[:, lanes])
        mod = k_ref[:, lanes] * (1.0 + (rate - 1.0) * vec[1:2])
        bonus = head_sum(r * mod * vec[2:3]) * v
        mixer_ref[:, lanes] = ((unit * vec[3:4] + vec[4:5] + bonus) * gate_ref[:, lanes]).astype(BF)


def whole(n=1):
    return [pl.BlockSpec(memory_space=pltpu.VMEM)] * n


def finish_forward(place, others, reach, out, r, k, v, rp, gate, vec):
    count, local = r.shape
    pairs = local // PAIR
    return pl.pallas_call(
        finish_kernel,
        in_specs=[pl.BlockSpec(memory_space=pltpu.SMEM)] + whole(len(others) + 8),
        out_specs=whole(3),
        out_shape=[
            jax.ShapeDtypeStruct((count, local), BF),
            jax.ShapeDtypeStruct((count, local), FL),
            jax.ShapeDtypeStruct((pairs, HEAD, PAIR), FL),
        ],
        name="finish_forward",
    )(place, *others, reach, out, r, k, v, rp, gate, vec)


def head_back_kernel(
    grad_ref, mixed_ref, reach_ref, r_ref, k_ref, v_ref, rp_ref, gate_ref, vec_ref,
    dy_ref, dgate_ref, ds_ref, sums_ref, state_ref,
):
    vec = vec_ref[...]
    grad, y, r, v, gate = grad_ref[...], mixed_ref[...], r_ref[...], v_ref[...], gate_ref[...]
    unit, scale = group_norm(y, vec)
    rate = jax.nn.sigmoid(rp_ref[...])
    mod = k_ref[...] * (1.0 + (rate - 1.0) * vec[1:2])
    dot_sum = head_sum(r * mod * vec[2:3])
    q = grad * gate
    dunit = q * vec[3:4]
    dy = scale * (
        dunit - head_sum(dunit) * (1.0 / HEAD) - unit * (head_sum(dunit * unit) * (1.0 / HEAD))
    )
    dy_ref[...] = dy
    full = mm(reach_ref[...], dy, TN)
    state_ref[0] = squeeze(jnp.where(same_head(PAIR, HEAD), full, 0.0)).astype(BF)
    dgate_ref[...] = grad * (unit * vec[3:4] + vec[4:5] + dot_sum * v)
    dsum = head_sum(q * v)
    ds_ref[...] = dsum
    row = lambda x: jnp.sum(x, 0, keepdims=True)
    zero = jnp.zeros((5, PAIR), FL)
    sums_ref[...] = jnp.concatenate([row(dsum * r * mod), row(q * unit), row(q), zero], 0)


def head_back(grad, mixed, reach, r, k, v, rp, gate, vec):
    count, local = r.shape
    pairs = local // PAIR
    return pl.pallas_call(
        head_back_kernel,
        grid=(pairs,),
        in_specs=[pair_spec(count)] * 8 + [pair_spec(8)],
        out_specs=[pair_spec(count)] * 3 + [pair_spec(8), block_spec(HEAD, PAIR)],
        out_shape=[jax.ShapeDtypeStruct((count, local), FL)] * 3
        + [
            jax.ShapeDtypeStruct((8, local), FL),
            jax.ShapeDtypeStruct((pairs, HEAD, PAIR), BF),
        ],
        name="head_back",
    )(grad, mixed, reach, r, k, v, rp, gate, vec)


def leave_kernel(place_ref, *refs):
    half = (len(refs) - 1) // 2
    moves, adds, out_ref = refs[:half], refs[half:-1], refs[-1]
    place = place_ref[0]
    size = half + 1
    for p in range(out_ref.shape[0]):
        state = jnp.zeros((PAIR, PAIR), FL)
        for ahead in range(half, 0, -1):
            slot = size - ahead - 1
            move = spread(moves[slot][p, 0].astype(FL)).astype(BF)
            high, low = parts(state)
            new = dot(move, high, TN) + dot(move, low, TN) + spread(adds[slot][p].astype(FL))
            state = jnp.where(place + ahead < size, new, 0.0)
        out_ref[p] = squeeze(state)


def leave_grad(place, moves, adds):
    pairs = adds[0].shape[0]
    return pl.pallas_call(
        leave_kernel,
        in_specs=[pl.BlockSpec(memory_space=pltpu.SMEM)] + whole(len(moves) + len(adds)),
        out_specs=whole(1)[0],
        out_shape=jax.ShapeDtypeStruct((pairs, HEAD, PAIR), FL),
        name="leave_grad",
    )(place, *moves, *adds)


def scan_back_kernel(
    grad_ref, dy_ref, ds_ref, r_ref, k_ref, v_ref, dp_ref, rp_ref, gate_ref, vec_ref,
    inverse_ref, enter_ref, leave_ref,
    dr_ref, dk_ref, dv_ref, ddp_ref, drp_ref, sums_ref,
):
    vec = vec_ref[...]
    r, k, v = r_ref[...], k_ref[...], v_ref[...]
    count = r.shape[0]
    span = span_of(count)
    chunks = count // span
    sig, logd, rate, inv_norm, unit, mod, removal = prepare(r, k, v, dp_ref[...], rp_ref[...], vec)
    dsum = ds_ref[...]
    state = spread(enter_ref[0])
    kept = []
    for index in range(chunks):
        at = slice(index * span, (index + 1) * span)
        q = chunk_of(r[at], v[at], logd[at], unit[at], mod[at], removal[at])
        inverse = parts(spread(inverse_ref[0, index]))
        vs, hs = parts(q["v"]), parts(state)
        along = mm(inverse, mm(q["ue"], hs) + mm(q["uk"], vs))
        kept.append((at, q, inverse, vs, state, hs, along))
        if index + 1 < chunks:
            end = jnp.sum(diagonal(q["end"]), 1, keepdims=True)
            state = end * state + mm(q["kd"], vs, TN) - mm(q["bd"], along, TN)
    leave = spread(leave_ref[0])
    tails = []
    for at, q, inverse, vs, state, hs, along in reversed(kept):
        dy = parts(spread(dy_ref[at, :]))
        lp = parts(leave)
        along_p = parts(along)
        kd, bd = parts(q["kd"]), parts(q["bd"])
        dalong = -(mm(q["rb"], dy, TN) + mm(bd, lp))
        z = mm(inverse, dalong, TN)
        zp = parts(z)
        dv = mm(q["rk"], dy, TN) + mm(kd, lp) + mm(q["uk"], zp, TN)
        end = jnp.sum(diagonal(q["end"]), 1, keepdims=True)
        ue, re, kl, bl = parts(q["ue"]), parts(q["re"]), parts(q["kl"]), parts(q["bl"])
        dstate = end * leave + mm(re, dy, TN) + mm(ue, zp, TN)
        rk = parts(jnp.where(q["inclusive"], mm(dy, vs, NT), 0.0))
        rb = parts(jnp.where(q["inclusive"], -mm(dy, along_p, NT), 0.0))
        uk = parts(jnp.where(q["strict"], mm(zp, vs, NT), 0.0))
        ub = parts(jnp.where(q["strict"], -mm(zp, along_p, NT), 0.0))
        dre = mm(dy, hs, NT) + mm(rk, kl) + mm(rb, bl)
        due = mm(zp, hs, NT) + mm(uk, kl) + mm(ub, bl)
        dkl = mm(rk, re, TN) + mm(uk, ue, TN)
        dbl = mm(rb, re, TN) + mm(ub, ue, TN)
        dkd = mm(vs, lp, NT)
        dbd = -mm(along_p, lp, NT)
        inside = squeeze(dre * q["re"] - dkl * q["kl"] - dbl * q["bl"] - dkd * q["kd"] - dbd * q["bd"])
        early = squeeze(due * q["ue"])
        ends = jnp.sum(squeeze(dkd * q["kd"] + dbd * q["bd"]), 0, keepdims=True)
        ones = jnp.ones((8, PAIR), BF)
        ends = ends + mm_ones(ones, state * leave, NT)[0:1] * q["end"]
        dlog = (
            mm_ones(tri(span, False, True).astype(FL).astype(BF), inside)
            + mm_ones(tri(span, True, True).astype(FL).astype(BF), early)
            + ends
        )
        dr = squeeze(dre) * q["c"]
        dunit = squeeze(due) * q["before"]
        dmod = squeeze(dkl) * q["inverse"] + squeeze(dkd) * q["ratio"]
        dremoval = squeeze(dbl) * q["inverse"] + squeeze(dbd) * q["ratio"]
        leave = dstate
        r_, k_, v_, rate_, mod_, unit_ = r[at], k[at], v[at], rate[at], mod[at], unit[at]
        bonus = dsum[at] * vec[2:3]
        dot_sum = head_sum(r_ * mod_ * vec[2:3])
        dr_ref[at, :] = (dr + bonus * mod_).astype(BF)
        dv_ref[at, :] = (squeeze(dv) + grad_ref[at, :] * gate_ref[at, :] * dot_sum).astype(BF)
        dmod = dmod + bonus * r_
        drate = dremoval * unit_ + dmod * k_ * vec[1:2]
        dunit = dunit + dremoval * rate_
        dscaled = inv_norm[at] * (dunit - unit_ * head_sum(dunit * unit_))
        dk_ref[at, :] = (dmod * (1.0 + (rate_ - 1.0) * vec[1:2]) + dscaled * vec[0:1]).astype(BF)
        drp = drate * rate_ * (1.0 - rate_)
        ddp = dlog * (-DECAY_SCALE) * sig[at] * (1.0 - sig[at])
        drp_ref[at, :] = drp.astype(BF)
        ddp_ref[at, :] = ddp.astype(BF)
        row = lambda x: jnp.sum(x, 0, keepdims=True)
        tails.append(
            jnp.concatenate(
                [row(ddp), row(drp), row(dscaled * k_), row(dmod * k_ * (rate_ - 1.0)), jnp.zeros((4, PAIR), FL)],
                0,
            )
        )
    sums_ref[...] = sum(tails[1:], tails[0])


def scan_back(grad, dy, ds, r, k, v, dp, rp, gate, vec, inverse, enter, leave):
    count, local = r.shape
    pairs = local // PAIR
    span = span_of(count)
    chunks = count // span
    return pl.pallas_call(
        scan_back_kernel,
        grid=(pairs,),
        in_specs=[pair_spec(count)] * 9
        + [
            pair_spec(8),
            block_spec(chunks, span, 2 * span),
            block_spec(HEAD, PAIR),
            block_spec(HEAD, PAIR),
        ],
        out_specs=[pair_spec(count)] * 5 + [pair_spec(8)],
        out_shape=[jax.ShapeDtypeStruct((count, local), BF)] * 5
        + [jax.ShapeDtypeStruct((8, local), FL)],
        name="scan_back",
    )(grad, dy, ds, r, k, v, dp, rp, gate, vec, inverse, enter, leave)


def layer_norm(value, gain, bias):
    center = value - jnp.mean(value, -1, keepdims=True)
    spread_ = jnp.mean(center * center, -1, keepdims=True)
    return center * lax.rsqrt(spread_ + EPS_LN) * gain + bias


def norm_back(value, gain, grad):
    center = value - jnp.mean(value, -1, keepdims=True)
    scale = lax.rsqrt(jnp.mean(center * center, -1, keepdims=True) + EPS_LN)
    unit = center * scale
    weighted = grad * gain
    back = scale * (
        weighted
        - jnp.mean(weighted, -1, keepdims=True)
        - unit * jnp.mean(weighted * unit, -1, keepdims=True)
    )
    return back, jnp.sum(grad * unit, 0), jnp.sum(grad, 0)


def rounded(x):
    return lax.reduce_precision(x, 8, 7)


def body(inputs, cotangent, vectors, mix_w, out_w, down_w, up_w, key_w, value_w):
    seq, tp = lax.axis_size("seq"), lax.axis_size("tp")
    count = seq // 2
    place, t = lax.axis_index("seq"), lax.axis_index("tp")
    i, j = place // 2, place % 2
    rows, width = inputs.shape
    tokens = cotangent.shape[0]
    local = mix_w.shape[2]
    part = width // seq
    rank = down_w.shape[1]
    quarter = rank // tp
    cuts = (0, DECAY_RANK, DECAY_RANK + RATE_RANK, rank)

    def swap(x):
        return lax.ppermute(x, "seq", [(s, s ^ 1) for s in range(seq)])

    def shift(x, k):
        route = [(2 * a + b, 2 * ((a + k) % count) + b) for a in range(count) for b in range(2)]
        return lax.ppermute(x, "seq", route)

    def turn(x, k):
        return lax.ppermute(x, "seq", [(s, (s + k) % seq) for s in range(seq)])

    def shift_t(x, k):
        return lax.ppermute(x, "tp", [(a, (a + k) % tp) for a in range(tp)])

    def next_rows(x, step):
        total = seq * tp
        route = [(d, d + step) for d in range(total) if 0 <= d + step < total]
        return lax.ppermute(x, ("seq", "tp"), route)

    def pick(x, index):
        return lax.dynamic_index_in_dim(x, index, 0, False)

    def own_first(x, axis):
        return jnp.where(j == 0, x, jnp.flip(x, axis))

    def blocks_of(x):
        c, m = x.shape[:2]
        return own_first(x.reshape(c, m, count, 2, part).transpose(2, 0, 3, 1, 4), 2)

    def to_columns(b):
        slots = [pick(b, i)] + [shift(pick(b, (i + k) % count), k) for k in range(1, count)]
        return jnp.stack(slots)

    def spread_rows(x):
        c = x.shape[0]
        g = lax.all_gather(to_columns(blocks_of(x)), "tp")
        return g.transpose(2, 3, 1, 0, 4, 5).reshape(c, 2, count * tokens, part)

    def scatter_t(p):
        low = p.astype(BF)
        total = pick(p, t)
        for k in range(1, tp):
            total = total + shift_t(pick(low, (t + k) % tp), k).astype(FL)
        return total

    def collect_rows(p):
        c = p.shape[0]
        mine = scatter_t(p.reshape(c, 2, count, tp, rows, part).transpose(3, 2, 0, 1, 4, 5))
        slots = jnp.stack([mine[0]] + [shift(mine[k], -k) for k in range(1, count)])
        slots = lax.dynamic_slice_in_dim(
            jnp.concatenate([slots, slots], 0), (count - i) % count, count, 0
        )
        return own_first(slots, 2).transpose(1, 3, 0, 2, 4).reshape(c, rows, width)

    def reduce_i(p, exact_row=False):
        total = p[:tokens]
        for k in range(1, count):
            block = p[k * tokens : (k + 1) * tokens]
            sent = block.astype(BF)
            if exact_row:
                head = block[:16]
                rest = head - rounded(head)
                got = shift(jnp.concatenate([sent, rest.astype(BF)], 0), -k).astype(FL)
                first = got[:16] + got[tokens:]
                total = total + jnp.concatenate([first, got[16:tokens]], 0)
            else:
                total = total + shift(sent, -k).astype(FL)
        return total

    def gather_i(x):
        return jnp.concatenate([x] + [shift(x, k) for k in range(1, count)], 0)

    def halves(x, *w):
        return dot(x[0], w[0], NN) + dot(x[1], w[1], NN)

    resid = inputs.astype(FL)
    before_rows = next_rows(inputs[-1:], 1)
    mix_n = swap(mix_w)
    down_o = lax.all_gather(down_w, "tp", axis=0, tiled=True)
    down_n = swap(down_o)
    up_n = swap(up_w)
    up_pair = jnp.where(j == 0, jnp.concatenate([up_w, up_n], 0), jnp.concatenate([up_n, up_w], 0))
    up_slots = jnp.stack([up_pair] + [shift(up_pair, k) for k in range(1, count)])[::-1]
    up = lax.dynamic_slice_in_dim(
        jnp.concatenate([up_slots, up_slots], 0), count - 1 - i, count, 0
    ).reshape(rank, local)
    value_n = swap(value_w)
    key_n = swap(key_w)
    full_out = lax.all_gather(out_w, "seq", axis=1, tiled=True)
    columns = lax.dynamic_slice_in_dim(vectors, t * local, local, 1)
    kernel_vec = jnp.concatenate([columns[12:17], jnp.zeros((3, local), FL)], 0)
    vec_block = own_first(pick(vectors.reshape(18, count, 2, part).transpose(1, 0, 2, 3), i), 1)

    def normed_one(x):
        return layer_norm(x.astype(FL), vectors[0], vectors[1]).astype(BF)

    normed1 = normed_one(inputs)
    is_first = (place == 0) & (t == 0)
    edge1 = jnp.where(is_first, jnp.zeros((), BF), normed_one(before_rows))
    shifted1 = jnp.concatenate([edge1, normed1[:-1]], 0)
    pair = spread_rows(jnp.stack([normed1, shifted1]))
    first = pair[0].astype(FL)
    delta1 = pair[1].astype(FL) - first
    mixes = [
        (first + delta1 * vec_block[4 + index][:, None, :]).astype(BF) for index in range(6)
    ]
    low = jnp.concatenate(
        [
            halves(m, down_o[:, a:b], down_n[:, a:b])
            for m, a, b in zip((mixes[1], mixes[4], mixes[5]), cuts, cuts[1:])
        ],
        1,
    )
    low = lax.dynamic_slice_in_dim(low, t * quarter, quarter, 1)
    partial = jnp.concatenate(
        [halves(mixes[m], mix_w[w], mix_n[w]) for w, m in enumerate((0, 2, 3))] + [low], 1
    )
    summed = reduce_i(partial, True)
    accept, keys, values = (summed[:, w * local : (w + 1) * local] for w in range(3))
    low = lax.all_gather(summed[:, 3 * local :], "tp", axis=1, tiled=True)
    tanh = jnp.tanh(low[:, : cuts[1]])
    gate_sig = jax.nn.sigmoid(low[:, cuts[2] :])
    hidden_low = (tanh.astype(BF), low[:, cuts[1] : cuts[2]].astype(BF), gate_sig.astype(BF))
    ups = [up[a:b] for a, b in zip(cuts, cuts[1:])]
    decay_pre = columns[10] + dot(hidden_low[0], ups[0], NN)
    rate_pre = columns[11] + dot(hidden_low[1], ups[1], NN)
    gate = dot(hidden_low[2], ups[2], NN)
    reach, local_out, state, inverse = local_scan(
        accept, keys, values, decay_pre, rate_pre, kernel_vec
    )
    place_ref = place.astype(jnp.int32).reshape(1)
    states = [turn(state, k) for k in range(1, seq)]
    mixer, mixed, enter = finish_forward(
        place_ref, states, reach, local_out, accept, keys, values, rate_pre, gate, kernel_vec
    )
    attended = scatter_t(dot(mixer, full_out, NN).reshape(tp, rows, width))
    middle = resid + attended

    cot_blocks = to_columns(blocks_of(cotangent[None]))
    cot2 = cot_blocks[:, 0].transpose(1, 0, 2, 3).reshape(2, count * tokens, part)
    grad_hidden = reduce_i(dot(cot2[0], value_w, NT) + dot(cot2[1], value_n, NT))
    normed2 = rounded(layer_norm(middle, vectors[2], vectors[3]))
    edge2 = next_rows(normed2[-1:].astype(BF), 1).astype(FL)
    delta2 = jnp.concatenate([edge2, normed2[:-1]], 0) - normed2
    ffn_rows = (normed2 + delta2 * vectors[17]).astype(BF)
    ffn2 = spread_rows(ffn_rows[None])[0]
    active = jax.nn.relu(reduce_i(halves(ffn2, key_w, key_n)))
    grad_pre = (grad_hidden * 2.0 * active).astype(BF)
    grad_pre2 = gather_i(grad_pre)
    hidden = (active * active).astype(BF)
    grad_ffn2 = jnp.stack([dot(grad_pre2, key_w, NT), dot(grad_pre2, key_n, NT)])
    grad_ffn = collect_rows(grad_ffn2[None])[0]
    carried2 = grad_ffn * vectors[17]
    spill2 = next_rows(carried2[:1], -1)
    grad_normed2 = grad_ffn * (1.0 - vectors[17]) + jnp.concatenate([carried2[1:], spill2], 0)
    mu_ffn = jnp.sum(grad_ffn * delta2, 0)
    norm_part, gain_two, bias_two = norm_back(middle, vectors[2], grad_normed2)
    cot_rows = lax.dynamic_slice_in_dim(cotangent, t * rows, rows, 0).astype(FL)
    grad_middle = cot_rows + norm_part
    middle_grad = lax.all_gather(grad_middle.astype(BF), "tp", axis=0, tiled=True)
    grad_mixer = dot(middle_grad, full_out, NT)

    dy, dgate, dsum, sums_a, state_grad = head_back(
        grad_mixer, mixed, reach, accept, keys, values, rate_pre, gate, kernel_vec
    )
    state_grads = [turn(state_grad, k) for k in range(1, seq)]
    leave = leave_grad(place_ref, states, state_grads)
    d_accept, d_keys, d_values, d_decay, d_rate, sums_b = scan_back(
        grad_mixer, dy, dsum, accept, keys, values, decay_pre, rate_pre, gate, kernel_vec,
        inverse, enter, leave,
    )
    d_gate = dgate.astype(BF)
    grads2 = [gather_i(g) for g in (d_accept, d_keys, d_values)]
    inner = jnp.concatenate(
        [dot(g, u, NT) for g, u in zip((d_decay, d_rate, d_gate), ups)], 1
    )
    slope = jnp.concatenate(
        [1.0 - tanh * tanh, jnp.ones((tokens, RATE_RANK), FL), gate_sig * (1.0 - gate_sig)], 1
    )
    inner = scatter_t(inner.reshape(tokens, tp, quarter).transpose(1, 0, 2))
    inner = (inner * lax.dynamic_slice_in_dim(slope, t * quarter, quarter, 1)).astype(BF)
    inner2 = lax.all_gather(gather_i(inner), "tp", axis=1, tiled=True)
    inners = [inner2[:, a:b] for a, b in zip(cuts, cuts[1:])]

    def mix_grad(half, index):
        w = (mix_w, mix_n)[half]
        d = (down_o, down_n)[half]
        if index in (0, 2, 3):
            at = (0, 2, 3).index(index)
            return dot(grads2[at], w[at], NT)
        at = (1, 4, 5).index(index)
        return dot(inners[at], d[:, cuts[at] : cuts[at + 1]], NT) * (1.0 / tp)

    carried, staying, mu_part = [], [], []
    for half in range(2):
        c1 = s1 = None
        mus = []
        for index in range(6):
            g = mix_grad(half, index)
            mu = vec_block[4 + index][half]
            c1 = g * mu if c1 is None else c1 + g * mu
            s1 = g * (1.0 - mu) if s1 is None else s1 + g * (1.0 - mu)
            mus.append(jnp.sum(g * delta1[half], 0))
        carried.append(c1)
        staying.append(s1)
        mu_part.append(jnp.stack(mus))
    both = collect_rows(jnp.stack([jnp.stack(staying), jnp.stack(carried)]))
    spill1 = next_rows(both[1][:1], -1)
    grad_normed1 = both[0] + jnp.concatenate([both[1][1:], spill1], 0)
    input_part, gain_one, bias_one = norm_back(resid, vectors[0], grad_normed1)
    grad_inputs = grad_middle + input_part

    hidden2 = gather_i(hidden)
    result2 = jnp.stack([dot(hidden2, value_w, NN), dot(hidden2, value_n, NN)])
    output = (middle + collect_rows(result2[None])[0]).astype(BF)

    def joined(own, other):
        return own + swap(other.astype(BF)).astype(FL)

    grad_value = joined(dot(hidden2, cot2[0], TN), dot(hidden2, cot2[1], TN))
    grad_key = joined(dot(ffn2[0], grad_pre2, TN), dot(ffn2[1], grad_pre2, TN))
    grad_out = lax.psum_scatter(
        dot(mixer, middle_grad, TN).astype(BF), "seq", scatter_dimension=1, tiled=True
    ).astype(FL)
    grad_mix = joined(
        *(
            jnp.stack([dot(mixes[m][half], g, TN) for m, g in zip((0, 2, 3), grads2)])
            for half in range(2)
        )
    )
    share = part // tp
    grad_down = joined(
        *(
            jnp.concatenate(
                [
                    dot(lax.dynamic_slice_in_dim(mixes[m][half], t * share, share, 1), g, TN)
                    for m, g in zip((1, 4, 5), inners)
                ],
                1,
            )
            for half in range(2)
        )
    )
    grad_up = lax.psum_scatter(
        jnp.concatenate(
            [dot(h, g, TN) for h, g in zip(hidden_low, (d_decay, d_rate, d_gate))], 0
        ).astype(BF),
        "seq",
        scatter_dimension=0,
        tiled=True,
    ).astype(FL)
    mu_rows = own_first(jnp.stack(mu_part, 1), 1).reshape(6, 2 * part)
    placed_mu = lax.dynamic_update_slice_in_dim(
        jnp.zeros((6, width), FL), mu_rows, i * 2 * part, 1
    )
    channel_rows = jnp.concatenate([sums_b[:4], sums_a[:3]], 0)
    placed = lax.dynamic_update_slice_in_dim(
        jnp.zeros((7, width), FL), channel_rows, t * local, 1
    )
    grad_vec = jnp.concatenate(
        [jnp.stack([gain_one, bias_one, gain_two, bias_two]), placed_mu, placed, mu_ffn[None]], 0
    )
    total = seq * tp
    grad_vec = grad_vec.reshape(18, total, width // total).transpose(1, 0, 2)
    grad_vec = jnp.sum(lax.all_to_all(grad_vec, ("seq", "tp"), 0, 0, tiled=True), 0)
    return (
        output,
        grad_inputs,
        grad_vec,
        grad_mix,
        grad_out,
        grad_down,
        grad_up,
        grad_key,
        grad_value,
    )


def solution(mesh):
    placed = (
        P(("seq", "tp"), None),
        P("seq", None),
        P(),
        P(None, "seq", "tp"),
        P("tp", "seq"),
        P(("seq", "tp"), None),
        P("seq", "tp"),
        P("seq", "tp"),
        P("tp", "seq"),
    )
    return jax.shard_map(
        body,
        mesh=mesh,
        in_specs=placed,
        out_specs=(
            P(("seq", "tp"), None),
            P(("seq", "tp"), None),
            P(None, ("seq", "tp")),
            P(None, "seq", "tp"),
            P("tp", "seq"),
            P(("seq", "tp"), None),
            P("seq", "tp"),
            P("seq", "tp"),
            P("tp", "seq"),
        ),
        check_vma=False,
    )
```

```python
import math

import jax
import jax.numpy as jnp
from jax import lax
from jax.experimental import pallas as pl
from jax.experimental.pallas import tpu as pltpu
from jax.sharding import PartitionSpec as P


HEAD = 64
PAIR = 2 * HEAD
DECAY_RANK = 96
RATE_RANK = 96
EPS_LN = 1e-05
EPS_GN = 0.00064
EPS_KEY = 1e-06
DECAY_SCALE = 0.606531
BF = jnp.bfloat16
FL = jnp.float32
NN = (((1,), (0,)), ((), ()))
NT = (((1,), (1,)), ((), ()))
TN = (((0,), (0,)), ((), ()))


def parts(a):
    if isinstance(a, tuple):
        return a
    high = a.astype(BF)
    return high, (a - high.astype(FL)).astype(BF)


def dot(a, b, dims):
    return lax.dot_general(a, b, dims, preferred_element_type=FL)


def mm(a, b, dims=NN):
    (ah, al), (bh, bl) = parts(a), parts(b)
    return dot(ah, bh, dims) + (dot(ah, bl, dims) + dot(al, bh, dims))


def mm_ones(ones, x, dims=NN):
    first = x.astype(BF)
    rest = x - first.astype(FL)
    second = rest.astype(BF)
    third = (rest - second.astype(FL)).astype(BF)
    return dot(ones, first, dims) + (dot(ones, second, dims) + dot(ones, third, dims))


def left_lanes(shape):
    return lax.broadcasted_iota(jnp.int32, shape, len(shape) - 1) < HEAD


def head_sum(x):
    mask = left_lanes(x.shape)
    left = jnp.sum(jnp.where(mask, x, 0.0), -1, keepdims=True)
    right = jnp.sum(jnp.where(mask, 0.0, x), -1, keepdims=True)
    return jnp.where(mask, left, right)


def spread(x):
    mask = left_lanes(x.shape)
    return jnp.concatenate([jnp.where(mask, x, 0.0), jnp.where(mask, 0.0, x)], 0)


def squeeze(x):
    half = x.shape[0] // 2
    return x[:half] + x[half:]


def same_head(rows, span):
    r = lax.broadcasted_iota(jnp.int32, (rows, PAIR), 0)
    c = lax.broadcasted_iota(jnp.int32, (rows, PAIR), 1)
    return (r >= span) == (c >= HEAD)


def prepare(k, dp, rp, vec):
    sig = jax.nn.sigmoid(dp)
    logd = -DECAY_SCALE * sig
    rate = jax.nn.sigmoid(rp)
    scaled = k * vec[0:1]
    inv_norm = lax.rsqrt(head_sum(scaled * scaled) + EPS_KEY)
    unit = scaled * inv_norm
    mod = k * (1.0 + (rate - 1.0) * vec[1:2])
    return sig, logd, rate, inv_norm, unit, mod, unit * rate


def tri(n, strict, upper=False):
    r = lax.broadcasted_iota(jnp.int32, (n, n), 0)
    c = lax.broadcasted_iota(jnp.int32, (n, n), 1)
    if upper:
        r, c = c, r
    return (r > c) if strict else (r >= c)


def chunk_of(r, v, logd, unit, mod, removal):
    span = r.shape[0]
    total = mm_ones(tri(span, False).astype(FL).astype(BF), logd)
    last = total[span - 1 : span]
    c, before, inverse, ratio = (
        jnp.exp(total),
        jnp.exp(total - logd),
        jnp.exp(-total),
        jnp.exp(last - total),
    )
    out = {
        "c": c,
        "before": before,
        "inverse": inverse,
        "ratio": ratio,
        "end": jnp.exp(last),
        "ue": spread(unit * before),
        "re": spread(r * c),
        "kl": spread(mod * inverse),
        "bl": spread(removal * inverse),
        "kd": spread(mod * ratio),
        "bd": spread(removal * ratio),
        "v": spread(v),
    }
    left = parts(jnp.concatenate([out["ue"], out["re"]], 0))
    right = parts(jnp.concatenate([out["bl"], out["kl"]], 0))
    both = mm(left, right, NT)
    rows = 2 * span
    r_id = lax.broadcasted_iota(jnp.int32, (rows, rows), 0)
    c_id = lax.broadcasted_iota(jnp.int32, (rows, rows), 1)
    head = (r_id >= span) == (c_id >= span)
    strict = head & (r_id > c_id)
    inclusive = head & (r_id >= c_id)
    out["strict"], out["inclusive"] = strict, inclusive
    out["ub"] = jnp.where(strict, both[:rows, :rows], 0.0)
    out["uk"] = jnp.where(strict, both[:rows, rows:], 0.0)
    out["rb"] = jnp.where(inclusive, both[rows:, :rows], 0.0)
    out["rk"] = jnp.where(inclusive, both[rows:, rows:], 0.0)
    return out


def unit_lower_inverse(lower, span):
    rows = lower.shape[0]
    r = lax.broadcasted_iota(jnp.int32, (rows, rows), 0)
    c = lax.broadcasted_iota(jnp.int32, (rows, rows), 1)
    result = None
    size = 1
    while size < span:
        select = (r // (2 * size) == c // (2 * size)) & (r // size != c // size)
        coupling = jnp.where(select, lower, 0.0)
        if result is None:
            result = jnp.where(r == c, 1.0, 0.0) - coupling
        else:
            split = parts(result)
            result = result - mm(split, mm(coupling, split))
        size *= 2
    return result


def diagonal(row):
    r = lax.broadcasted_iota(jnp.int32, (PAIR, PAIR), 0)
    c = lax.broadcasted_iota(jnp.int32, (PAIR, PAIR), 1)
    return jnp.where(r == c, row, 0.0)


def span_of(count):
    return math.gcd(count, HEAD)


def local_kernel(r_ref, k_ref, v_ref, dp_ref, rp_ref, vec_ref, reach_ref, out_ref, state_ref, inverse_ref):
    r, k, v = r_ref[...], k_ref[...], v_ref[...]
    count = r.shape[0]
    span = span_of(count)
    vec = vec_ref[...]
    _, logd, _, _, unit, mod, removal = prepare(k, dp_ref[...], rp_ref[...], vec)
    move = add = None
    for index in range(count // span):
        at = slice(index * span, (index + 1) * span)
        q = chunk_of(r[at], v[at], logd[at], unit[at], mod[at], removal[at])
        inverse = unit_lower_inverse(q["ub"], span)
        inverse_ref[0, index] = squeeze(inverse)
        vs = parts(q["v"])
        side = mm(inverse, jnp.concatenate([q["ue"], mm(q["uk"], vs)], 1))
        side = parts(side)
        read = mm(q["rb"], side)
        reach = q["re"] - read[:, :PAIR]
        local = mm(q["rk"], vs) - read[:, PAIR:]
        gone = mm(q["bd"], side, TN)
        step_move = diagonal(q["end"]) - gone[:, :PAIR]
        step_add = mm(q["kd"], vs, TN) - gone[:, PAIR:]
        if index == 0:
            move, add = step_move, step_add
        else:
            so_far = parts(jnp.concatenate([move, add], 1))
            both = mm(reach, so_far)
            reach, local = both[:, :PAIR], local + both[:, PAIR:]
            both = mm(step_move, so_far)
            move, add = both[:, :PAIR], step_add + both[:, PAIR:]
        reach_ref[at, :] = squeeze(reach)
        out_ref[at, :] = squeeze(local)
    state_ref[0, 0] = squeeze(move).astype(BF)
    state_ref[0, 1] = squeeze(add).astype(BF)


def pair_spec(rows):
    return pl.BlockSpec((rows, PAIR), lambda p: (0, p))


def block_spec(*lead):
    return pl.BlockSpec((1, *lead), lambda p: (p,) + (0,) * len(lead))


def local_scan(r, k, v, dp, rp, vec):
    count, local = r.shape
    pairs, chunks = local // PAIR, count // span_of(count)
    span = span_of(count)
    return pl.pallas_call(
        local_kernel,
        grid=(pairs,),
        in_specs=[pair_spec(count)] * 5 + [pair_spec(8)],
        out_specs=[
            pair_spec(count),
            pair_spec(count),
            block_spec(2, HEAD, PAIR),
            block_spec(chunks, span, 2 * span),
        ],
        out_shape=[
            jax.ShapeDtypeStruct((count, local), FL),
            jax.ShapeDtypeStruct((count, local), FL),
            jax.ShapeDtypeStruct((pairs, 2, HEAD, PAIR), BF),
            jax.ShapeDtypeStruct((pairs, chunks, span, 2 * span), FL),
        ],
        name="local_scan",
    )(r, k, v, dp, rp, vec)


def group_norm(y):
    center = y - head_sum(y) * (1.0 / HEAD)
    scale = lax.rsqrt(head_sum(center * center) * (1.0 / HEAD) + EPS_GN)
    return center * scale, scale


def finish_kernel(place_ref, *refs):
    others, (reach_ref, out_ref, r_ref, k_ref, v_ref, rp_ref, gate_ref, vec_ref), (
        mixer_ref,
        mixed_ref,
        enter_ref,
    ) = refs[:-11], refs[-11:-3], refs[-3:]
    place = place_ref[0]
    seen = len(others)
    for p in range(reach_ref.shape[1] // PAIR):
        lanes = slice(p * PAIR, (p + 1) * PAIR)
        state = jnp.zeros((PAIR, PAIR), FL)
        for k in range(seen, 0, -1):
            slot = others[k - 1]
            move = spread(slot[p, 0].astype(FL)).astype(BF)
            high, low = parts(state)
            new = dot(move, high, NN) + dot(move, low, NN) + spread(slot[p, 1].astype(FL))
            state = jnp.where(k <= place, new, 0.0)
        enter_ref[p] = squeeze(state)
        vec = vec_ref[:, lanes]
        r, v = r_ref[:, lanes], v_ref[:, lanes]
        y = out_ref[:, lanes] + mm(reach_ref[:, lanes], state)
        mixed_ref[:, lanes] = y
        unit, _ = group_norm(y)
        rate = jax.nn.sigmoid(rp_ref[:, lanes])
        mod = k_ref[:, lanes] * (1.0 + (rate - 1.0) * vec[1:2])
        bonus = head_sum(r * mod * vec[2:3]) * v
        mixer_ref[:, lanes] = ((unit * vec[3:4] + vec[4:5] + bonus) * gate_ref[:, lanes]).astype(BF)


def whole(n=1):
    return [pl.BlockSpec(memory_space=pltpu.VMEM)] * n


def finish_forward(place, others, reach, out, r, k, v, rp, gate, vec):
    count, local = r.shape
    pairs = local // PAIR
    return pl.pallas_call(
        finish_kernel,
        in_specs=[pl.BlockSpec(memory_space=pltpu.SMEM)] + whole(len(others) + 8),
        out_specs=whole(3),
        out_shape=[
            jax.ShapeDtypeStruct((count, local), BF),
            jax.ShapeDtypeStruct((count, local), FL),
            jax.ShapeDtypeStruct((pairs, HEAD, PAIR), FL),
        ],
        name="finish_forward",
    )(place, *others, reach, out, r, k, v, rp, gate, vec)


def head_back_kernel(
    grad_ref, mixed_ref, reach_ref, r_ref, k_ref, v_ref, rp_ref, gate_ref, vec_ref,
    dy_ref, dgate_ref, ds_ref, sums_ref, state_ref,
):
    vec = vec_ref[...]
    grad, y, r, v, gate = grad_ref[...], mixed_ref[...], r_ref[...], v_ref[...], gate_ref[...]
    unit, scale = group_norm(y)
    rate = jax.nn.sigmoid(rp_ref[...])
    mod = k_ref[...] * (1.0 + (rate - 1.0) * vec[1:2])
    dot_sum = head_sum(r * mod * vec[2:3])
    q = grad * gate
    dunit = q * vec[3:4]
    dy = scale * (
        dunit - head_sum(dunit) * (1.0 / HEAD) - unit * (head_sum(dunit * unit) * (1.0 / HEAD))
    )
    dy_ref[...] = dy
    full = mm(reach_ref[...], dy, TN)
    state_ref[0] = squeeze(jnp.where(same_head(PAIR, HEAD), full, 0.0)).astype(BF)
    dgate_ref[...] = grad * (unit * vec[3:4] + vec[4:5] + dot_sum * v)
    dsum = head_sum(q * v)
    ds_ref[...] = dsum
    row = lambda x: jnp.sum(x, 0, keepdims=True)
    zero = jnp.zeros((5, PAIR), FL)
    sums_ref[...] = jnp.concatenate([row(dsum * r * mod), row(q * unit), row(q), zero], 0)


def head_back(grad, mixed, reach, r, k, v, rp, gate, vec):
    count, local = r.shape
    pairs = local // PAIR
    return pl.pallas_call(
        head_back_kernel,
        grid=(pairs,),
        in_specs=[pair_spec(count)] * 8 + [pair_spec(8)],
        out_specs=[pair_spec(count)] * 3 + [pair_spec(8), block_spec(HEAD, PAIR)],
        out_shape=[jax.ShapeDtypeStruct((count, local), FL)] * 3
        + [
            jax.ShapeDtypeStruct((8, local), FL),
            jax.ShapeDtypeStruct((pairs, HEAD, PAIR), BF),
        ],
        name="head_back",
    )(grad, mixed, reach, r, k, v, rp, gate, vec)


def leave_kernel(place_ref, *refs):
    half = (len(refs) - 1) // 2
    moves, adds, out_ref = refs[:half], refs[half:-1], refs[-1]
    place = place_ref[0]
    size = half + 1
    for p in range(out_ref.shape[0]):
        state = jnp.zeros((PAIR, PAIR), FL)
        for ahead in range(half, 0, -1):
            slot = size - ahead - 1
            move = spread(moves[slot][p, 0].astype(FL)).astype(BF)
            high, low = parts(state)
            new = dot(move, high, TN) + dot(move, low, TN) + spread(adds[slot][p].astype(FL))
            state = jnp.where(place + ahead < size, new, 0.0)
        out_ref[p] = squeeze(state)


def leave_grad(place, moves, adds):
    pairs = adds[0].shape[0]
    return pl.pallas_call(
        leave_kernel,
        in_specs=[pl.BlockSpec(memory_space=pltpu.SMEM)] + whole(len(moves) + len(adds)),
        out_specs=whole(1)[0],
        out_shape=jax.ShapeDtypeStruct((pairs, HEAD, PAIR), FL),
        name="leave_grad",
    )(place, *moves, *adds)


def scan_back_kernel(
    grad_ref, dy_ref, ds_ref, r_ref, k_ref, v_ref, dp_ref, rp_ref, gate_ref, vec_ref,
    inverse_ref, enter_ref, leave_ref,
    dr_ref, dk_ref, dv_ref, ddp_ref, drp_ref, sums_ref,
):
    vec = vec_ref[...]
    r, k, v = r_ref[...], k_ref[...], v_ref[...]
    count = r.shape[0]
    span = span_of(count)
    chunks = count // span
    sig, logd, rate, inv_norm, unit, mod, removal = prepare(k, dp_ref[...], rp_ref[...], vec)
    dsum = ds_ref[...]
    state = spread(enter_ref[0])
    kept = []
    for index in range(chunks):
        at = slice(index * span, (index + 1) * span)
        q = chunk_of(r[at], v[at], logd[at], unit[at], mod[at], removal[at])
        inverse = parts(spread(inverse_ref[0, index]))
        vs, hs = parts(q["v"]), parts(state)
        along = mm(inverse, mm(q["ue"], hs) + mm(q["uk"], vs))
        kept.append((at, q, inverse, vs, state, hs, along))
        if index + 1 < chunks:
            end = jnp.sum(diagonal(q["end"]), 1, keepdims=True)
            state = end * state + mm(q["kd"], vs, TN) - mm(q["bd"], along, TN)
    leave = spread(leave_ref[0])
    tails = []
    for at, q, inverse, vs, state, hs, along in reversed(kept):
        dy = parts(spread(dy_ref[at, :]))
        lp = parts(leave)
        along_p = parts(along)
        kd, bd = parts(q["kd"]), parts(q["bd"])
        dalong = -(mm(q["rb"], dy, TN) + mm(bd, lp))
        z = mm(inverse, dalong, TN)
        zp = parts(z)
        dv = mm(q["rk"], dy, TN) + mm(kd, lp) + mm(q["uk"], zp, TN)
        end = jnp.sum(diagonal(q["end"]), 1, keepdims=True)
        ue, re, kl, bl = parts(q["ue"]), parts(q["re"]), parts(q["kl"]), parts(q["bl"])
        dstate = end * leave + mm(re, dy, TN) + mm(ue, zp, TN)
        rk = parts(jnp.where(q["inclusive"], mm(dy, vs, NT), 0.0))
        rb = parts(jnp.where(q["inclusive"], -mm(dy, along_p, NT), 0.0))
        uk = parts(jnp.where(q["strict"], mm(zp, vs, NT), 0.0))
        ub = parts(jnp.where(q["strict"], -mm(zp, along_p, NT), 0.0))
        dre = mm(dy, hs, NT) + mm(rk, kl) + mm(rb, bl)
        due = mm(zp, hs, NT) + mm(uk, kl) + mm(ub, bl)
        dkl = mm(rk, re, TN) + mm(uk, ue, TN)
        dbl = mm(rb, re, TN) + mm(ub, ue, TN)
        dkd = mm(vs, lp, NT)
        dbd = -mm(along_p, lp, NT)
        inside = squeeze(dre * q["re"] - dkl * q["kl"] - dbl * q["bl"] - dkd * q["kd"] - dbd * q["bd"])
        early = squeeze(due * q["ue"])
        ends = jnp.sum(squeeze(dkd * q["kd"] + dbd * q["bd"]), 0, keepdims=True)
        ones = jnp.ones((8, PAIR), BF)
        ends = ends + mm_ones(ones, state * leave, NT)[0:1] * q["end"]
        dlog = (
            mm_ones(tri(span, False, True).astype(FL).astype(BF), inside)
            + mm_ones(tri(span, True, True).astype(FL).astype(BF), early)
            + ends
        )
        dr = squeeze(dre) * q["c"]
        dunit = squeeze(due) * q["before"]
        dmod = squeeze(dkl) * q["inverse"] + squeeze(dkd) * q["ratio"]
        dremoval = squeeze(dbl) * q["inverse"] + squeeze(dbd) * q["ratio"]
        leave = dstate
        r_, k_, rate_, mod_, unit_ = r[at], k[at], rate[at], mod[at], unit[at]
        bonus = dsum[at] * vec[2:3]
        dot_sum = head_sum(r_ * mod_ * vec[2:3])
        dr_ref[at, :] = (dr + bonus * mod_).astype(BF)
        dv_ref[at, :] = (squeeze(dv) + grad_ref[at, :] * gate_ref[at, :] * dot_sum).astype(BF)
        dmod = dmod + bonus * r_
        drate = dremoval * unit_ + dmod * k_ * vec[1:2]
        dunit = dunit + dremoval * rate_
        dscaled = inv_norm[at] * (dunit - unit_ * head_sum(dunit * unit_))
        dk_ref[at, :] = (dmod * (1.0 + (rate_ - 1.0) * vec[1:2]) + dscaled * vec[0:1]).astype(BF)
        drp = drate * rate_ * (1.0 - rate_)
        ddp = dlog * (-DECAY_SCALE) * sig[at] * (1.0 - sig[at])
        drp_ref[at, :] = drp.astype(BF)
        ddp_ref[at, :] = ddp.astype(BF)
        row = lambda x: jnp.sum(x, 0, keepdims=True)
        tails.append(
            jnp.concatenate(
                [row(ddp), row(drp), row(dscaled * k_), row(dmod * k_ * (rate_ - 1.0)), jnp.zeros((4, PAIR), FL)],
                0,
            )
        )
    sums_ref[...] = sum(tails[1:], tails[0])


def scan_back(grad, dy, ds, r, k, v, dp, rp, gate, vec, inverse, enter, leave):
    count, local = r.shape
    pairs = local // PAIR
    span = span_of(count)
    chunks = count // span
    return pl.pallas_call(
        scan_back_kernel,
        grid=(pairs,),
        in_specs=[pair_spec(count)] * 9
        + [
            pair_spec(8),
            block_spec(chunks, span, 2 * span),
            block_spec(HEAD, PAIR),
            block_spec(HEAD, PAIR),
        ],
        out_specs=[pair_spec(count)] * 5 + [pair_spec(8)],
        out_shape=[jax.ShapeDtypeStruct((count, local), BF)] * 5
        + [jax.ShapeDtypeStruct((8, local), FL)],
        name="scan_back",
    )(grad, dy, ds, r, k, v, dp, rp, gate, vec, inverse, enter, leave)


def layer_norm(value, gain, bias):
    center = value - jnp.mean(value, -1, keepdims=True)
    spread_ = jnp.mean(center * center, -1, keepdims=True)
    return center * lax.rsqrt(spread_ + EPS_LN) * gain + bias


def norm_back(value, gain, grad):
    center = value - jnp.mean(value, -1, keepdims=True)
    scale = lax.rsqrt(jnp.mean(center * center, -1, keepdims=True) + EPS_LN)
    unit = center * scale
    weighted = grad * gain
    back = scale * (
        weighted
        - jnp.mean(weighted, -1, keepdims=True)
        - unit * jnp.mean(weighted * unit, -1, keepdims=True)
    )
    return back, jnp.sum(grad * unit, 0), jnp.sum(grad, 0)


def rounded(x):
    return lax.reduce_precision(x, 8, 7)


def block(inputs, cotangent, vectors, mix_w, out_w, down_w, up_w, key_w, value_w):
    seq, tp = lax.axis_size("seq"), lax.axis_size("tp")
    count = seq // 2
    place, t = lax.axis_index("seq"), lax.axis_index("tp")
    i, j = place // 2, place % 2
    rows, width = inputs.shape
    tokens = cotangent.shape[0]
    local = mix_w.shape[2]
    part = width // seq
    rank = down_w.shape[1]
    quarter = rank // tp
    cuts = (0, DECAY_RANK, DECAY_RANK + RATE_RANK, rank)

    def swap(x):
        return lax.ppermute(x, "seq", [(s, s ^ 1) for s in range(seq)])

    def shift(x, k):
        route = [(2 * a + b, 2 * ((a + k) % count) + b) for a in range(count) for b in range(2)]
        return lax.ppermute(x, "seq", route)

    def turn(x, k):
        return lax.ppermute(x, "seq", [(s, (s + k) % seq) for s in range(seq)])

    def shift_t(x, k):
        return lax.ppermute(x, "tp", [(a, (a + k) % tp) for a in range(tp)])

    def next_rows(x, step):
        total = seq * tp
        route = [(d, d + step) for d in range(total) if 0 <= d + step < total]
        return lax.ppermute(x, ("seq", "tp"), route)

    def pick(x, index):
        return lax.dynamic_index_in_dim(x, index, 0, False)

    def own_first(x, axis):
        return jnp.where(j == 0, x, jnp.flip(x, axis))

    def blocks_of(x):
        c, m = x.shape[:2]
        return own_first(x.reshape(c, m, count, 2, part).transpose(2, 0, 3, 1, 4), 2)

    def to_columns(b):
        slots = [pick(b, i)] + [shift(pick(b, (i + k) % count), k) for k in range(1, count)]
        return jnp.stack(slots)

    def spread_rows(x):
        c = x.shape[0]
        g = lax.all_gather(to_columns(blocks_of(x)), "tp")
        return g.transpose(2, 3, 1, 0, 4, 5).reshape(c, 2, count * tokens, part)

    def scatter_t(p):
        low = p.astype(BF)
        total = pick(p, t)
        for k in range(1, tp):
            total = total + shift_t(pick(low, (t + k) % tp), k).astype(FL)
        return total

    def collect_rows(p):
        c = p.shape[0]
        mine = scatter_t(p.reshape(c, 2, count, tp, rows, part).transpose(3, 2, 0, 1, 4, 5))
        slots = jnp.stack([mine[0]] + [shift(mine[k], -k) for k in range(1, count)])
        slots = lax.dynamic_slice_in_dim(
            jnp.concatenate([slots, slots], 0), (count - i) % count, count, 0
        )
        return own_first(slots, 2).transpose(1, 3, 0, 2, 4).reshape(c, rows, width)

    def reduce_i(p, exact_row=False):
        total = p[:tokens]
        for k in range(1, count):
            block = p[k * tokens : (k + 1) * tokens]
            sent = block.astype(BF)
            if exact_row:
                head = block[:16]
                rest = head - rounded(head)
                got = shift(jnp.concatenate([sent, rest.astype(BF)], 0), -k).astype(FL)
                first = got[:16] + got[tokens:]
                total = total + jnp.concatenate([first, got[16:tokens]], 0)
            else:
                total = total + shift(sent, -k).astype(FL)
        return total

    def gather_i(x):
        return jnp.concatenate([x] + [shift(x, k) for k in range(1, count)], 0)

    def halves(x, *w):
        return dot(x[0], w[0], NN) + dot(x[1], w[1], NN)

    resid = inputs.astype(FL)
    before_rows = next_rows(inputs[-1:], 1)
    mix_n = swap(mix_w)
    down_o = lax.all_gather(down_w, "tp", axis=0, tiled=True)
    down_n = swap(down_o)
    up_n = swap(up_w)
    up_pair = jnp.where(j == 0, jnp.concatenate([up_w, up_n], 0), jnp.concatenate([up_n, up_w], 0))
    up_slots = jnp.stack([up_pair] + [shift(up_pair, k) for k in range(1, count)])[::-1]
    up = lax.dynamic_slice_in_dim(
        jnp.concatenate([up_slots, up_slots], 0), count - 1 - i, count, 0
    ).reshape(rank, local)
    value_n = swap(value_w)
    key_n = swap(key_w)
    full_out = lax.all_gather(out_w, "seq", axis=1, tiled=True)
    columns = lax.dynamic_slice_in_dim(vectors, t * local, local, 1)
    kernel_vec = jnp.concatenate([columns[12:17], jnp.zeros((3, local), FL)], 0)
    vec_block = own_first(pick(vectors.reshape(18, count, 2, part).transpose(1, 0, 2, 3), i), 1)

    def normed_one(x):
        return layer_norm(x.astype(FL), vectors[0], vectors[1]).astype(BF)

    normed1 = normed_one(inputs)
    is_first = (place == 0) & (t == 0)
    edge1 = jnp.where(is_first, jnp.zeros((), BF), normed_one(before_rows))
    shifted1 = jnp.concatenate([edge1, normed1[:-1]], 0)
    pair = spread_rows(jnp.stack([normed1, shifted1]))
    first = pair[0].astype(FL)
    delta1 = pair[1].astype(FL) - first
    mixes = [
        (first + delta1 * vec_block[4 + index][:, None, :]).astype(BF) for index in range(6)
    ]
    low = jnp.concatenate(
        [
            halves(m, down_o[:, a:b], down_n[:, a:b])
            for m, a, b in zip((mixes[1], mixes[4], mixes[5]), cuts, cuts[1:])
        ],
        1,
    )
    low = lax.dynamic_slice_in_dim(low, t * quarter, quarter, 1)
    partial = jnp.concatenate(
        [halves(mixes[m], mix_w[w], mix_n[w]) for w, m in enumerate((0, 2, 3))] + [low], 1
    )
    summed = reduce_i(partial, True)
    accept, keys, values = (summed[:, w * local : (w + 1) * local] for w in range(3))
    low = lax.all_gather(summed[:, 3 * local :], "tp", axis=1, tiled=True)
    tanh = jnp.tanh(low[:, : cuts[1]])
    gate_sig = jax.nn.sigmoid(low[:, cuts[2] :])
    hidden_low = (tanh.astype(BF), low[:, cuts[1] : cuts[2]].astype(BF), gate_sig.astype(BF))
    ups = [up[a:b] for a, b in zip(cuts, cuts[1:])]
    decay_pre = columns[10] + dot(hidden_low[0], ups[0], NN)
    rate_pre = columns[11] + dot(hidden_low[1], ups[1], NN)
    gate = dot(hidden_low[2], ups[2], NN)
    reach, local_out, state, inverse = local_scan(
        accept, keys, values, decay_pre, rate_pre, kernel_vec
    )
    place_ref = place.astype(jnp.int32).reshape(1)
    states = [turn(state, k) for k in range(1, seq)]
    mixer, mixed, enter = finish_forward(
        place_ref, states, reach, local_out, accept, keys, values, rate_pre, gate, kernel_vec
    )
    attended = scatter_t(dot(mixer, full_out, NN).reshape(tp, rows, width))
    middle = resid + attended

    cot_blocks = to_columns(blocks_of(cotangent[None]))
    cot2 = cot_blocks[:, 0].transpose(1, 0, 2, 3).reshape(2, count * tokens, part)
    grad_hidden = reduce_i(dot(cot2[0], value_w, NT) + dot(cot2[1], value_n, NT))
    normed2 = rounded(layer_norm(middle, vectors[2], vectors[3]))
    edge2 = next_rows(normed2[-1:].astype(BF), 1).astype(FL)
    delta2 = jnp.concatenate([edge2, normed2[:-1]], 0) - normed2
    ffn_rows = (normed2 + delta2 * vectors[17]).astype(BF)
    ffn2 = spread_rows(ffn_rows[None])[0]
    active = jax.nn.relu(reduce_i(halves(ffn2, key_w, key_n)))
    grad_pre = (grad_hidden * 2.0 * active).astype(BF)
    grad_pre2 = gather_i(grad_pre)
    hidden = (active * active).astype(BF)
    grad_ffn2 = jnp.stack([dot(grad_pre2, key_w, NT), dot(grad_pre2, key_n, NT)])
    grad_ffn = collect_rows(grad_ffn2[None])[0]
    carried2 = grad_ffn * vectors[17]
    spill2 = next_rows(carried2[:1], -1)
    grad_normed2 = grad_ffn * (1.0 - vectors[17]) + jnp.concatenate([carried2[1:], spill2], 0)
    mu_ffn = jnp.sum(grad_ffn * delta2, 0)
    norm_part, gain_two, bias_two = norm_back(middle, vectors[2], grad_normed2)
    cot_rows = lax.dynamic_slice_in_dim(cotangent, t * rows, rows, 0).astype(FL)
    grad_middle = cot_rows + norm_part
    middle_grad = lax.all_gather(grad_middle.astype(BF), "tp", axis=0, tiled=True)
    grad_mixer = dot(middle_grad, full_out, NT)

    dy, dgate, dsum, sums_a, state_grad = head_back(
        grad_mixer, mixed, reach, accept, keys, values, rate_pre, gate, kernel_vec
    )
    state_grads = [turn(state_grad, k) for k in range(1, seq)]
    leave = leave_grad(place_ref, states, state_grads)
    d_accept, d_keys, d_values, d_decay, d_rate, sums_b = scan_back(
        grad_mixer, dy, dsum, accept, keys, values, decay_pre, rate_pre, gate, kernel_vec,
        inverse, enter, leave,
    )
    d_gate = dgate.astype(BF)
    grads2 = [gather_i(g) for g in (d_accept, d_keys, d_values)]
    inner = jnp.concatenate(
        [dot(g, u, NT) for g, u in zip((d_decay, d_rate, d_gate), ups)], 1
    )
    slope = jnp.concatenate(
        [1.0 - tanh * tanh, jnp.ones((tokens, RATE_RANK), FL), gate_sig * (1.0 - gate_sig)], 1
    )
    inner = scatter_t(inner.reshape(tokens, tp, quarter).transpose(1, 0, 2))
    inner = (inner * lax.dynamic_slice_in_dim(slope, t * quarter, quarter, 1)).astype(BF)
    inner2 = lax.all_gather(gather_i(inner), "tp", axis=1, tiled=True)
    inners = [inner2[:, a:b] for a, b in zip(cuts, cuts[1:])]

    def mix_grad(half, index):
        w = (mix_w, mix_n)[half]
        d = (down_o, down_n)[half]
        if index in (0, 2, 3):
            at = (0, 2, 3).index(index)
            return dot(grads2[at], w[at], NT)
        at = (1, 4, 5).index(index)
        return dot(inners[at], d[:, cuts[at] : cuts[at + 1]], NT) * (1.0 / tp)

    carried, staying, mu_part = [], [], []
    for half in range(2):
        c1 = s1 = None
        mus = []
        for index in range(6):
            g = mix_grad(half, index)
            mu = vec_block[4 + index][half]
            c1 = g * mu if c1 is None else c1 + g * mu
            s1 = g * (1.0 - mu) if s1 is None else s1 + g * (1.0 - mu)
            mus.append(jnp.sum(g * delta1[half], 0))
        carried.append(c1)
        staying.append(s1)
        mu_part.append(jnp.stack(mus))
    both = collect_rows(jnp.stack([jnp.stack(staying), jnp.stack(carried)]))
    spill1 = next_rows(both[1][:1], -1)
    grad_normed1 = both[0] + jnp.concatenate([both[1][1:], spill1], 0)
    input_part, gain_one, bias_one = norm_back(resid, vectors[0], grad_normed1)
    grad_inputs = grad_middle + input_part

    hidden_slots = [hidden] + [shift(hidden, k) for k in range(1, count)]
    hidden_slots, _ = lax.optimization_barrier((hidden_slots, d_accept))
    hidden2 = jnp.concatenate(hidden_slots, 0)
    result2 = jnp.stack([dot(hidden2, value_w, NN), dot(hidden2, value_n, NN)])
    output = (middle + collect_rows(result2[None])[0]).astype(BF)

    def joined(own, other):
        return own + swap(other.astype(BF)).astype(FL)

    grad_value = joined(dot(hidden2, cot2[0], TN), dot(hidden2, cot2[1], TN))
    grad_key = joined(dot(ffn2[0], grad_pre2, TN), dot(ffn2[1], grad_pre2, TN))
    grad_out = lax.psum_scatter(
        dot(mixer, middle_grad, TN).astype(BF), "seq", scatter_dimension=1, tiled=True
    ).astype(FL)
    grad_mix = joined(
        *(
            jnp.stack([dot(mixes[m][half], g, TN) for m, g in zip((0, 2, 3), grads2)])
            for half in range(2)
        )
    )
    share = part // tp
    grad_down = joined(
        *(
            jnp.concatenate(
                [
                    dot(lax.dynamic_slice_in_dim(mixes[m][half], t * share, share, 1), g, TN)
                    for m, g in zip((1, 4, 5), inners)
                ],
                1,
            )
            for half in range(2)
        )
    )
    grad_up = lax.psum_scatter(
        jnp.concatenate(
            [dot(h, g, TN) for h, g in zip(hidden_low, (d_decay, d_rate, d_gate))], 0
        ).astype(BF),
        "seq",
        scatter_dimension=0,
        tiled=True,
    ).astype(FL)
    mu_rows = own_first(jnp.stack(mu_part, 1), 1).reshape(6, 2 * part)
    placed_mu = lax.dynamic_update_slice_in_dim(
        jnp.zeros((6, width), FL), mu_rows, i * 2 * part, 1
    )
    channel_rows = jnp.concatenate([sums_b[:4], sums_a[:3]], 0)
    placed = lax.dynamic_update_slice_in_dim(
        jnp.zeros((7, width), FL), channel_rows, t * local, 1
    )
    grad_vec = jnp.concatenate(
        [jnp.stack([gain_one, bias_one, gain_two, bias_two]), placed_mu, placed, mu_ffn[None]], 0
    )
    total = seq * tp
    grad_vec = grad_vec.reshape(18, total, width // total).transpose(1, 0, 2)
    grad_vec = jnp.sum(lax.all_to_all(grad_vec, ("seq", "tp"), 0, 0, tiled=True), 0)
    return (
        output,
        grad_inputs,
        grad_vec,
        grad_mix,
        grad_out,
        grad_down,
        grad_up,
        grad_key,
        grad_value,
    )


def solution(mesh):
    placed = (
        P(("seq", "tp"), None),
        P("seq", None),
        P(),
        P(None, "seq", "tp"),
        P("tp", "seq"),
        P(("seq", "tp"), None),
        P("seq", "tp"),
        P("seq", "tp"),
        P("tp", "seq"),
    )
    return jax.shard_map(
        block,
        mesh=mesh,
        in_specs=placed,
        out_specs=(
            P(("seq", "tp"), None),
            P(("seq", "tp"), None),
            P(None, ("seq", "tp")),
            P(None, "seq", "tp"),
            P("tp", "seq"),
            P(("seq", "tp"), None),
            P("seq", "tp"),
            P("seq", "tp"),
            P("tp", "seq"),
        ),
        check_vma=False,
    )
```

```python
import functools
import itertools
import math

import jax
import jax.numpy as jnp
from jax import lax
from jax.experimental import pallas as pl
from jax.experimental.pallas import tpu as pltpu
from jax.sharding import PartitionSpec as P


HEAD = 64
PAIR = 2 * HEAD
DECAY_RANK = 96
RATE_RANK = 96
EPS_LN = 1e-05
EPS_GN = 0.00064
EPS_KEY = 1e-06
DECAY_SCALE = 0.606531
BF = jnp.bfloat16
FL = jnp.float32
NN = (((1,), (0,)), ((), ()))
NT = (((1,), (1,)), ((), ()))
TN = (((0,), (0,)), ((), ()))


def parts(a):
    if isinstance(a, tuple):
        return a
    high = a.astype(BF)
    return high, (a - high.astype(FL)).astype(BF)


def dot(a, b, dims):
    return lax.dot_general(a, b, dims, preferred_element_type=FL)


def mm(a, b, dims=NN):
    (ah, al), (bh, bl) = parts(a), parts(b)
    return dot(ah, bh, dims) + (dot(ah, bl, dims) + dot(al, bh, dims))


def mm_ones(ones, x, dims=NN):
    first = x.astype(BF)
    rest = x - first.astype(FL)
    second = rest.astype(BF)
    third = (rest - second.astype(FL)).astype(BF)
    return dot(ones, first, dims) + (dot(ones, second, dims) + dot(ones, third, dims))


def left_lanes(shape):
    return lax.broadcasted_iota(jnp.int32, shape, len(shape) - 1) < HEAD


def head_sum(x):
    mask = left_lanes(x.shape)
    left = jnp.sum(jnp.where(mask, x, 0.0), -1, keepdims=True)
    right = jnp.sum(jnp.where(mask, 0.0, x), -1, keepdims=True)
    return jnp.where(mask, left, right)


def spread(x):
    mask = left_lanes(x.shape)
    return jnp.concatenate([jnp.where(mask, x, 0.0), jnp.where(mask, 0.0, x)], 0)


def squeeze(x):
    half = x.shape[0] // 2
    return x[:half] + x[half:]


def same_head(rows, span):
    r = lax.broadcasted_iota(jnp.int32, (rows, PAIR), 0)
    c = lax.broadcasted_iota(jnp.int32, (rows, PAIR), 1)
    return (r >= span) == (c >= HEAD)


def prepare(k, dp, rp, vec):
    sig = jax.nn.sigmoid(dp)
    logd = -DECAY_SCALE * sig
    rate = jax.nn.sigmoid(rp)
    scaled = k * vec[0:1]
    inv_norm = lax.rsqrt(head_sum(scaled * scaled) + EPS_KEY)
    unit = scaled * inv_norm
    mod = k * (1.0 + (rate - 1.0) * vec[1:2])
    return sig, logd, rate, inv_norm, unit, mod, unit * rate


def tri(n, strict, upper=False):
    r = lax.broadcasted_iota(jnp.int32, (n, n), 0)
    c = lax.broadcasted_iota(jnp.int32, (n, n), 1)
    if upper:
        r, c = c, r
    return (r > c) if strict else (r >= c)


def chunk_of(r, v, logd, unit, mod, removal):
    span = r.shape[0]
    total = mm_ones(tri(span, False).astype(FL).astype(BF), logd)
    last = total[span - 1 : span]
    c, before, inverse, ratio = (
        jnp.exp(total),
        jnp.exp(total - logd),
        jnp.exp(-total),
        jnp.exp(last - total),
    )
    out = {
        "c": c,
        "before": before,
        "inverse": inverse,
        "ratio": ratio,
        "end": jnp.exp(last),
        "ue": spread(unit * before),
        "re": spread(r * c),
        "kl": spread(mod * inverse),
        "bl": spread(removal * inverse),
        "kd": spread(mod * ratio),
        "bd": spread(removal * ratio),
        "v": spread(v),
    }
    left = parts(jnp.concatenate([out["ue"], out["re"]], 0))
    right = parts(jnp.concatenate([out["bl"], out["kl"]], 0))
    both = mm(left, right, NT)
    rows = 2 * span
    r_id = lax.broadcasted_iota(jnp.int32, (rows, rows), 0)
    c_id = lax.broadcasted_iota(jnp.int32, (rows, rows), 1)
    head = (r_id >= span) == (c_id >= span)
    strict = head & (r_id > c_id)
    inclusive = head & (r_id >= c_id)
    out["strict"], out["inclusive"] = strict, inclusive
    out["ub"] = jnp.where(strict, both[:rows, :rows], 0.0)
    out["uk"] = jnp.where(strict, both[:rows, rows:], 0.0)
    out["rb"] = jnp.where(inclusive, both[rows:, :rows], 0.0)
    out["rk"] = jnp.where(inclusive, both[rows:, rows:], 0.0)
    return out


def unit_lower_inverse(lower, span):
    rows = lower.shape[0]
    r = lax.broadcasted_iota(jnp.int32, (rows, rows), 0)
    c = lax.broadcasted_iota(jnp.int32, (rows, rows), 1)
    result = None
    size = 1
    while size < span:
        select = (r // (2 * size) == c // (2 * size)) & (r // size != c // size)
        coupling = jnp.where(select, lower, 0.0)
        if result is None:
            result = jnp.where(r == c, 1.0, 0.0) - coupling
        else:
            split = parts(result)
            result = result - mm(split, mm(coupling, split))
        size *= 2
    return result


def diagonal(row):
    r = lax.broadcasted_iota(jnp.int32, (PAIR, PAIR), 0)
    c = lax.broadcasted_iota(jnp.int32, (PAIR, PAIR), 1)
    return jnp.where(r == c, row, 0.0)


def span_of(count):
    return math.gcd(count, HEAD)


def full(shape):
    return pl.BlockSpec(shape, lambda *_: (0,) * len(shape))


SCALARS = pl.BlockSpec(memory_space=pltpu.SMEM)


def shaped(*shape, dtype=FL):
    return jax.ShapeDtypeStruct(shape, dtype)


def run(kernel, scalars, ins, outs, scratch=()):
    return pl.pallas_call(
        kernel,
        in_specs=[SCALARS] + [full(x.shape) for x in ins],
        out_specs=[full(x.shape) for x in outs],
        out_shape=list(outs),
        scratch_shapes=list(scratch),
    )(scalars, *ins)


def norm_parts(value):
    center = value - jnp.mean(value, -1, keepdims=True)
    scale = lax.rsqrt(jnp.mean(center * center, -1, keepdims=True) + EPS_LN)
    return center * scale, scale


def norm_back(value, gain, grad):
    unit, scale = norm_parts(value)
    weighted = grad * gain
    back = scale * (
        weighted
        - jnp.mean(weighted, -1, keepdims=True)
        - unit * jnp.mean(weighted * unit, -1, keepdims=True)
    )
    return back, jnp.sum(grad * unit, 0, keepdims=True), jnp.sum(grad, 0, keepdims=True)


def row_id(x):
    return lax.broadcasted_iota(jnp.int32, x.shape, 0)


def after(x, edge):
    return jnp.where(row_id(x) == 0, edge, pltpu.roll(x, 1, 0))


def before(x, edge):
    last = x.shape[0] - 1
    return jnp.where(row_id(x) == last, edge, pltpu.roll(x, last, 0))


def cut_columns(values, store_ref, outs, i, j):
    count = len(outs)
    part = store_ref.shape[-1]
    for c, x in enumerate(values):
        for b in range(count):
            for half in range(2):
                at = (2 * b + half) * part
                store_ref[b, c, lax.rem(half + j, 2)] = x[:, at : at + part]
    for k in range(count):
        outs[k][...] = store_ref[lax.rem(i + k, count)]


def rows_in_kernel(s_ref, x_ref, edge_ref, vec_ref, *refs):
    outs, store_ref = refs[:-1], refs[-1]
    gain, bias = vec_ref[0:1], vec_ref[1:2]

    def normed(x):
        return (norm_parts(x.astype(FL))[0] * gain + bias).astype(BF)

    own = normed(x_ref[...])
    edge = normed(edge_ref[...]).astype(FL)
    edge = jnp.where(s_ref[3] == 1, 0.0, edge)
    prior = after(own.astype(FL), edge).astype(BF)
    cut_columns((own, prior), store_ref, outs, s_ref[0], s_ref[1])


def split_kernel(s_ref, x_ref, *refs):
    cut_columns((x_ref[...],), refs[-1], refs[:-1], s_ref[0], s_ref[1])


def join_kernel(s_ref, *refs):
    for k, ref in enumerate(refs[:-1]):
        refs[-1][k] = ref[...]


def stacked(g_ref, k, *at):
    return jnp.concatenate([g_ref[(q, k, *at)] for q in range(g_ref.shape[0])], 0)


def mixes_of(g_ref, vec_ref, k, half):
    first = stacked(g_ref, k, 0, half).astype(FL)
    delta = stacked(g_ref, k, 1, half).astype(FL) - first
    return delta, [(first + delta * vec_ref[half, c : c + 1]).astype(BF) for c in range(6)]


def low_masks(shape):
    lane = lax.broadcasted_iota(jnp.int32, shape, 1)
    first, second = DECAY_RANK, DECAY_RANK + RATE_RANK
    return lane < first, (lane >= first) & (lane < second), lane >= second


def only(mask, x):
    return jnp.where(mask, x.astype(FL), 0.0).astype(x.dtype)


def mix_forward_kernel(s_ref, g_ref, vec_ref, wo_ref, wn_ref, do_ref, dn_ref, own_ref, *refs):
    sent, low_ref = refs[:-1], refs[-1]
    tokens = own_ref.shape[0]
    local = wo_ref.shape[2]
    quarter = own_ref.shape[1] - 3 * local
    weights, downs = (wo_ref, wn_ref), (do_ref, dn_ref)
    masks = low_masks(do_ref.shape)
    masked = [[only(m, d[...]) for m in masks] for d in downs]
    for k in range(len(sent) + 1):
        sums = [None] * 4
        for half in range(2):
            _, mixes = mixes_of(g_ref, vec_ref, k, half)
            new = [dot(mixes[m], weights[half][w], NN) for w, m in enumerate((0, 2, 3))]
            new.append(sum(dot(mixes[m], masked[half][q], NN) for q, m in enumerate((1, 4, 5))))
            sums = new if sums[0] is None else [a + b for a, b in zip(sums, new)]
        low_ref[...] = sums[3]
        sums[3] = low_ref[:, pl.ds(pl.multiple_of(s_ref[2] * quarter, quarter), quarter)]
        at = 0
        for x in sums:
            lanes = slice(at, at + x.shape[1])
            at += x.shape[1]
            if k == 0:
                own_ref[:, lanes] = x
            else:
                high = x.astype(BF)
                sent[k - 1][:tokens, lanes] = high
                sent[k - 1][tokens:, lanes] = (x[:16] - high[:16].astype(FL)).astype(BF)


def total_of(own, others):
    tokens = own.shape[0]
    for x in others:
        x = x.astype(FL)
        own = own + x[:tokens]
        low = jnp.concatenate([x[tokens:], jnp.zeros((tokens - 16, x.shape[1]), FL)], 0)
        own = own + low
    return own


def emit_rows(buf_ref, own_ref, sent, t):
    rows = own_ref.shape[-2]
    tp = len(sent) + 1
    lead = buf_ref.shape[:-2]
    for m in range(tp):
        at = pl.ds(pl.multiple_of(lax.rem(t + m, tp) * rows, rows), rows)
        for index in itertools.product(*(range(d) for d in lead)):
            x = buf_ref[(*index, at, slice(None))]
            if m == 0:
                own_ref[index] = x
            else:
                sent[m - 1][index] = x.astype(BF)


def collect_kernel(s_ref, own_ref, *refs):
    count = own_ref.shape[1]
    others, outs = refs[:-count], refs[-count:]
    for k in range(count):
        total = own_ref[:, k]
        for ref in others:
            total = total + ref[:, k].astype(FL)
        outs[k][...] = total


def assemble(slots, store_ref, i, j):
    count = len(slots)
    channels = slots[0].shape[0]
    for k, ref in enumerate(slots):
        for half in range(2):
            store_ref[lax.rem(i + k, count), lax.rem(half + j, 2)] = ref[:, half]
    return [
        jnp.concatenate([store_ref[b, half, c] for b in range(count) for half in range(2)], 1)
        for c in range(channels)
    ]


def rows_mid_kernel(s_ref, x_ref, vec_ref, own_ref, *refs):
    others, (middle_ref, normed_ref, last_ref) = refs[:-3], refs[-3:]
    attended = own_ref[...]
    for ref in others:
        attended = attended + ref[...].astype(FL)
    middle = x_ref[...].astype(FL) + attended
    middle_ref[...] = middle
    normed = (norm_parts(middle)[0] * vec_ref[2:3] + vec_ref[3:4]).astype(BF)
    normed_ref[...] = normed
    last_ref[...] = normed[normed.shape[0] - 1 :]


def rows_ffn_kernel(s_ref, normed_ref, edge_ref, vec_ref, *refs):
    normed = normed_ref[...].astype(FL)
    delta = after(normed, edge_ref[...].astype(FL)) - normed
    x = (normed + delta * vec_ref[17:18]).astype(BF)
    cut_columns((x,), refs[-1], refs[:-1], s_ref[0], s_ref[1])


def rows_back_kernel(s_ref, vec_ref, *refs):
    slots, (grad_ref, edge_ref, store_ref) = refs[:-3], refs[-3:]
    (grad,) = assemble(slots, store_ref, s_ref[0], s_ref[1])
    grad_ref[...] = grad
    edge_ref[...] = grad[0:1] * vec_ref[17:18]


def middle_back_kernel(
    s_ref, grad_ref, next_ref, middle_ref, normed_ref, edge_ref, cot_ref, vec_ref,
    out_ref, low_ref, sums_ref,
):
    grad = grad_ref[...]
    mu = vec_ref[17:18]
    normed = normed_ref[...].astype(FL)
    delta = after(normed, edge_ref[...].astype(FL)) - normed
    shifted = before(grad * mu, next_ref[...])
    back, gain, bias = norm_back(middle_ref[...], vec_ref[2:3], grad * (1.0 - mu) + shifted)
    rows = out_ref.shape[0]
    at = pl.ds(pl.multiple_of(s_ref[2] * rows, rows), rows)
    total = cot_ref[at, :].astype(FL) + back
    out_ref[...] = total
    low_ref[...] = total.astype(BF)
    sums_ref[0:1] = gain
    sums_ref[1:2] = bias
    sums_ref[2:3] = jnp.sum(grad * delta, 0, keepdims=True)


def first_back_kernel(s_ref, x_ref, both_s_ref, both_c_ref, next_ref, middle_ref, vec_ref, out_ref, sums_ref):
    grad = both_s_ref[...] + before(both_c_ref[...], next_ref[...])
    back, gain, bias = norm_back(x_ref[...].astype(FL), vec_ref[0:1], grad)
    out_ref[...] = middle_ref[...] + back
    sums_ref[0:1] = gain
    sums_ref[1:2] = bias


def rows_two_kernel(s_ref, *refs):
    slots, (stay_ref, carry_ref, edge_ref, store_ref) = refs[:-4], refs[-4:]
    stay, carry = assemble(slots, store_ref, s_ref[0], s_ref[1])
    stay_ref[...] = stay
    carry_ref[...] = carry
    edge_ref[...] = carry[0:1]


def output_kernel(s_ref, middle_ref, *refs):
    slots, (out_ref, store_ref) = refs[:-2], refs[-2:]
    (rows,) = assemble(slots, store_ref, s_ref[0], s_ref[1])
    out_ref[...] = (middle_ref[...] + rows).astype(BF)


def grid_block(width):
    for size in (640, 512, 256, 128):
        if width % size == 0:
            return size
    return width


def key_kernel(g_ref, ko_ref, kn_ref, own_ref, *sent):
    for k in range(len(sent) + 1):
        x = dot(stacked(g_ref, k, 0, 0), ko_ref[...], NN) + dot(stacked(g_ref, k, 0, 1), kn_ref[...], NN)
        if k == 0:
            own_ref[...] = x
        else:
            sent[k - 1][...] = x.astype(BF)


def products(kernel, ins, specs, tokens, width, count):
    size = grid_block(width)
    block = pl.BlockSpec((tokens, size), lambda q: (0, q))
    return pl.pallas_call(
        kernel,
        grid=(width // size,),
        in_specs=specs(size),
        out_specs=[block] * count,
        out_shape=[shaped(tokens, width)] + [shaped(tokens, width, dtype=BF)] * (count - 1),
    )(*ins)


def key_forward(g, own_w, next_w):
    tp, count, _, _, rows, part = g.shape
    return products(
        key_kernel,
        (g, own_w, next_w),
        lambda size: [full(g.shape)] + [pl.BlockSpec((part, size), lambda q: (0, q))] * 2,
        tp * rows,
        own_w.shape[1],
        count,
    )


def value_kernel(*refs):
    count = (len(refs) - 2) // 2
    cots, vo_ref, vn_ref, own_ref, sent = (
        refs[:count], refs[count], refs[count + 1], refs[count + 2], refs[count + 3 :],
    )
    for k, cot_ref in enumerate(cots):
        x = dot(cot_ref[0, 0], vo_ref[...], NT) + dot(cot_ref[0, 1], vn_ref[...], NT)
        if k == 0:
            own_ref[...] = x
        else:
            sent[k - 1][...] = x.astype(BF)


def value_back(cots, own_w, next_w):
    count = len(cots)
    _, _, tokens, part = cots[0].shape
    return products(
        value_kernel,
        (*cots, own_w, next_w),
        lambda size: [full(c.shape) for c in cots]
        + [pl.BlockSpec((size, part), lambda q: (q, 0))] * 2,
        tokens,
        own_w.shape[0],
        count,
    )


def ffn_back_kernel(count, dims, s_ref, *refs):
    slots, (wo_ref, wn_ref, own_ref), sent, buf_ref = (
        refs[:count], refs[count : count + 3], refs[count + 3 : -1], refs[-1],
    )
    step = pl.program_id(0)
    for k, slot in enumerate(slots):
        for half, w in enumerate((wo_ref, wn_ref)):
            new = dot(slot[...], w[...], dims)

            @pl.when(step == 0)
            def _():
                buf_ref[0, k, half] = new

            @pl.when(step > 0)
            def _():
                buf_ref[0, k, half] += new

    @pl.when(step == pl.num_programs(0) - 1)
    def _():
        emit_rows(buf_ref, own_ref, sent, s_ref[2])


def ffn_back(scalars, slots, own_w, next_w, transposed, tp):
    count = len(slots)
    tokens, width = slots[0].shape
    rows = tokens // tp
    size = grid_block(width)
    part = own_w.shape[0] if transposed else own_w.shape[1]
    weight = (
        pl.BlockSpec((part, size), lambda q: (0, q))
        if transposed
        else pl.BlockSpec((size, part), lambda q: (q, 0))
    )
    shape = (1, count, 2, rows, part)
    return pl.pallas_call(
        functools.partial(ffn_back_kernel, count, NT if transposed else NN),
        grid=(width // size,),
        in_specs=[SCALARS]
        + [pl.BlockSpec((tokens, size), lambda q: (0, q))] * count
        + [weight] * 2,
        out_specs=[full(shape)] * tp,
        out_shape=[shaped(*shape)] + [shaped(*shape, dtype=BF)] * (tp - 1),
        scratch_shapes=[pltpu.VMEM((1, count, 2, tokens, part), FL)],
    )(scalars, *slots, own_w, next_w)


def key_grad_kernel(count, g_ref, *refs):
    slots, (own_ref, next_ref) = refs[:count], refs[count:]
    for half, out in enumerate((own_ref, next_ref)):
        total = sum(dot(stacked(g_ref, k, 0, half), s[...], TN) for k, s in enumerate(slots))
        out[...] = total.astype(out.dtype)


def key_grad(g, slots):
    _, count, _, _, _, part = g.shape
    tokens, width = slots[0].shape
    size = grid_block(width)
    out = pl.BlockSpec((part, size), lambda q: (0, q))
    return pl.pallas_call(
        functools.partial(key_grad_kernel, count),
        grid=(width // size,),
        in_specs=[full(g.shape)] + [pl.BlockSpec((tokens, size), lambda q: (0, q))] * count,
        out_specs=[out, out],
        out_shape=[shaped(part, width), shaped(part, width, dtype=BF)],
        name="key_grad",
    )(g, *slots)


def value_grad_kernel(count, *refs):
    slots, cots, (own_ref, next_ref) = refs[:count], refs[count : 2 * count], refs[2 * count :]
    for half, out in enumerate((own_ref, next_ref)):
        total = sum(dot(s[...], c[0, half], TN) for s, c in zip(slots, cots))
        out[...] = total.astype(out.dtype)


def value_grad(slots, cots):
    count = len(slots)
    tokens, width = slots[0].shape
    part = cots[0].shape[-1]
    size = grid_block(width)
    out = pl.BlockSpec((size, part), lambda q: (q, 0))
    return pl.pallas_call(
        functools.partial(value_grad_kernel, count),
        grid=(width // size,),
        in_specs=[pl.BlockSpec((tokens, size), lambda q: (0, q))] * count
        + [full(c.shape) for c in cots],
        out_specs=[out, out],
        out_shape=[shaped(width, part), shaped(width, part, dtype=BF)],
        name="value_grad",
    )(*slots, *cots)


def lora_back_kernel(s_ref, low_ref, up_ref, dd_ref, dr_ref, dg_ref, own_ref, *refs):
    sent, (grad_ref, buf_ref) = refs[:-2], refs[-2:]
    low = jnp.concatenate([low_ref[q] for q in range(low_ref.shape[0])], 1)
    masks = low_masks(low.shape)
    grads = (dd_ref[...], dr_ref[...], dg_ref[...].astype(BF))
    acts = (jnp.tanh(low), low, jax.nn.sigmoid(low))
    inner = 0.0
    total = 0.0
    for mask, act, grad in zip(masks, acts, grads):
        inner = jnp.where(mask, dot(grad, up_ref[...], NT), inner)
        total = total + dot(only(mask, act.astype(BF)), grad, TN)
    slope = jnp.where(masks[0], 1.0 - acts[0] * acts[0], 1.0)
    slope = jnp.where(masks[2], acts[2] * (1.0 - acts[2]), slope)
    grad_ref[...] = total.astype(BF)
    buf_ref[...] = inner * slope
    tp = len(sent) + 1
    quarter = own_ref.shape[1]
    for m in range(tp):
        x = buf_ref[:, pl.ds(pl.multiple_of(lax.rem(s_ref[2] + m, tp) * quarter, quarter), quarter)]
        if m == 0:
            own_ref[...] = x
        else:
            sent[m - 1][...] = x.astype(BF)


def inner_of(inner_ref, k):
    return jnp.concatenate([inner_ref[q, k] for q in range(inner_ref.shape[0])], 1)


def mix_back_kernel(count, s_ref, g_ref, vec_ref, inner_ref, *refs):
    grads = [refs[w * count : (w + 1) * count] for w in range(3)]
    wo_ref, wn_ref, do_ref, dn_ref, own_ref = refs[3 * count : 3 * count + 5]
    sent, (mu_ref, buf_ref) = refs[3 * count + 5 : -2], refs[-2:]
    weights, downs = (wo_ref, wn_ref), (do_ref, dn_ref)
    tp = len(sent) + 1
    masks = low_masks(do_ref.shape)
    masked = [[only(m, d[...]) for m in masks] for d in downs]
    for half in range(2):
        sums = [0.0] * 6
        for k in range(count):
            first = stacked(g_ref, k, 0, half).astype(FL)
            delta = stacked(g_ref, k, 1, half).astype(FL) - first
            inner = inner_of(inner_ref, k)
            stay = carry = 0.0
            for c in range(6):
                if c in (0, 2, 3):
                    w = (0, 2, 3).index(c)
                    g = dot(grads[w][k][...], weights[half][w], NT)
                else:
                    g = dot(inner, masked[half][(1, 4, 5).index(c)], NT) * (1.0 / tp)
                mu = vec_ref[half, c : c + 1]
                moved = g * mu
                carry = carry + moved
                stay = stay + (g - moved)
                sums[c] = sums[c] + jnp.sum(g * delta, 0, keepdims=True)
            buf_ref[0, k, half] = stay
            buf_ref[1, k, half] = carry
        for c in range(6):
            mu_ref[half, c : c + 1] = sums[c]
        mu_ref[half, 6:8] = jnp.zeros((2, mu_ref.shape[2]), FL)
    emit_rows(buf_ref, own_ref, sent, s_ref[2])


def mix_grad_kernel(count, s_ref, g_ref, vec_ref, inner_ref, *refs):
    grads = [refs[w * count : (w + 1) * count] for w in range(3)]
    outs, downs = refs[3 * count : 3 * count + 2], refs[3 * count + 2 :]
    for half in range(2):
        total = [0.0] * 4
        for k in range(count):
            _, mixes = mixes_of(g_ref, vec_ref, k, half)
            inner = inner_of(inner_ref, k)
            masks = low_masks(inner.shape)
            for w, m in enumerate((0, 2, 3)):
                total[w] = total[w] + dot(mixes[m], grads[w][k][...], TN)
            for q, m in enumerate((1, 4, 5)):
                total[3] = total[3] + dot(mixes[m], only(masks[q], inner), TN)
        for w in range(3):
            outs[half][w] = total[w].astype(outs[half].dtype)
        downs[half][...] = total[3].astype(downs[half].dtype)


def local_kernel(count, low_ref, up_ref, off_ref, vec_ref, *refs):
    sums, outs = refs[: 3 * count], refs[3 * count :]
    _, _, _, _, _, _, reach_ref, out_ref, state_ref, inverse_ref = outs
    r, k, v = (
        total_of(sums[w * count][...], [x[...] for x in sums[w * count + 1 : (w + 1) * count]])
        for w in range(3)
    )
    low = jnp.concatenate([low_ref[q] for q in range(low_ref.shape[0])], 1)
    acts = (jnp.tanh(low), low, jax.nn.sigmoid(low))
    dp, rp, gate = (
        dot(only(mask, act.astype(BF)), up_ref[...], NN) for mask, act in zip(low_masks(low.shape), acts)
    )
    dp, rp = dp + off_ref[0:1], rp + off_ref[1:2]
    for ref, x in zip(outs, (r, k, v, dp, rp, gate)):
        ref[...] = x
    count = r.shape[0]
    span = span_of(count)
    vec = vec_ref[...]
    _, logd, _, _, unit, mod, removal = prepare(k, dp, rp, vec)
    move = add = None
    for index in range(count // span):
        at = slice(index * span, (index + 1) * span)
        q = chunk_of(r[at], v[at], logd[at], unit[at], mod[at], removal[at])
        inverse = unit_lower_inverse(q["ub"], span)
        inverse_ref[0, index] = squeeze(inverse)
        vs = parts(q["v"])
        side = mm(inverse, jnp.concatenate([q["ue"], mm(q["uk"], vs)], 1))
        side = parts(side)
        read = mm(q["rb"], side)
        reach = q["re"] - read[:, :PAIR]
        local = mm(q["rk"], vs) - read[:, PAIR:]
        gone = mm(q["bd"], side, TN)
        step_move = diagonal(q["end"]) - gone[:, :PAIR]
        step_add = mm(q["kd"], vs, TN) - gone[:, PAIR:]
        if index == 0:
            move, add = step_move, step_add
        else:
            so_far = parts(jnp.concatenate([move, add], 1))
            both = mm(reach, so_far)
            reach, local = both[:, :PAIR], local + both[:, PAIR:]
            both = mm(step_move, so_far)
            move, add = both[:, :PAIR], step_add + both[:, PAIR:]
        reach_ref[at, :] = squeeze(reach)
        out_ref[at, :] = squeeze(local)
    state_ref[0, 0] = squeeze(move).astype(BF)
    state_ref[0, 1] = squeeze(add).astype(BF)


def pair_spec(rows):
    return pl.BlockSpec((rows, PAIR), lambda p: (0, p))


def block_spec(*lead):
    return pl.BlockSpec((1, *lead), lambda p: (p,) + (0,) * len(lead))


def local_scan(low, up, off, vec, own, others):
    tokens, local = own.shape[0], up.shape[1]
    pairs, chunks = local // PAIR, tokens // span_of(tokens)
    span = span_of(tokens)
    count = len(others) + 1
    specs = [
        pl.BlockSpec((x.shape[0], PAIR), functools.partial(lambda w, p: (0, w * pairs + p), w))
        for w in range(3)
        for x in (own, *others)
    ]
    return pl.pallas_call(
        functools.partial(local_kernel, count),
        grid=(pairs,),
        in_specs=[full(low.shape), pair_spec(up.shape[0]), pair_spec(2), pair_spec(8)] + specs,
        out_specs=[pair_spec(tokens)] * 8
        + [block_spec(2, HEAD, PAIR), block_spec(chunks, span, 2 * span)],
        out_shape=[jax.ShapeDtypeStruct((tokens, local), FL)] * 8
        + [
            jax.ShapeDtypeStruct((pairs, 2, HEAD, PAIR), BF),
            jax.ShapeDtypeStruct((pairs, chunks, span, 2 * span), FL),
        ],
        name="local_scan",
    )(low, up, off, vec, *([own, *others] * 3))


def group_norm(y):
    center = y - head_sum(y) * (1.0 / HEAD)
    scale = lax.rsqrt(head_sum(center * center) * (1.0 / HEAD) + EPS_GN)
    return center * scale, scale


def finish_kernel(seen, s_ref, *refs):
    others, refs = refs[:seen], refs[seen:]
    reach_ref, out_ref, r_ref, k_ref, v_ref, rp_ref, gate_ref, vec_ref, w_ref = refs[:9]
    mixer_ref, mixed_ref, enter_ref, own_ref = refs[9:13]
    sent, buf_ref = refs[13:-1], refs[-1]
    place = s_ref[4]
    for p in range(reach_ref.shape[1] // PAIR):
        lanes = slice(p * PAIR, (p + 1) * PAIR)
        state = jnp.zeros((PAIR, PAIR), FL)
        for k in range(seen, 0, -1):
            slot = others[k - 1]
            move = spread(slot[p, 0].astype(FL)).astype(BF)
            high, low = parts(state)
            new = dot(move, high, NN) + dot(move, low, NN) + spread(slot[p, 1].astype(FL))
            state = jnp.where(k <= place, new, 0.0)
        enter_ref[p] = squeeze(state)
        vec = vec_ref[:, lanes]
        r, v = r_ref[:, lanes], v_ref[:, lanes]
        y = out_ref[:, lanes] + mm(reach_ref[:, lanes], state)
        mixed_ref[:, lanes] = y
        unit, _ = group_norm(y)
        rate = jax.nn.sigmoid(rp_ref[:, lanes])
        mod = k_ref[:, lanes] * (1.0 + (rate - 1.0) * vec[1:2])
        bonus = head_sum(r * mod * vec[2:3]) * v
        mixer_ref[:, lanes] = ((unit * vec[3:4] + vec[4:5] + bonus) * gate_ref[:, lanes]).astype(BF)
    buf_ref[...] = dot(mixer_ref[...], w_ref[...], NN)
    rows = own_ref.shape[0]
    tp = len(sent) + 1
    for m in range(tp):
        x = buf_ref[pl.ds(pl.multiple_of(lax.rem(s_ref[2] + m, tp) * rows, rows), rows), :]
        if m == 0:
            own_ref[...] = x
        else:
            sent[m - 1][...] = x.astype(BF)


def whole(n=1):
    return [pl.BlockSpec(memory_space=pltpu.VMEM)] * n


def finish_forward(scalars, others, tp, *ins):
    tokens, local = ins[0].shape
    width = ins[-1].shape[1]
    rows = tokens // tp
    return run(
        functools.partial(finish_kernel, len(others)),
        scalars,
        (*others, *ins),
        [
            shaped(tokens, local, dtype=BF),
            shaped(tokens, local),
            shaped(local // PAIR, HEAD, PAIR),
            shaped(rows, width),
        ]
        + [shaped(rows, width, dtype=BF)] * (tp - 1),
        [pltpu.VMEM((tokens, width), FL)],
    )


def head_back_kernel(
    middle_ref, w_ref, mixed_ref, reach_ref, r_ref, k_ref, v_ref, rp_ref, gate_ref, vec_ref,
    grad_ref, dy_ref, dgate_ref, ds_ref, sums_ref, state_ref,
):
    vec = vec_ref[...]
    grad = dot(middle_ref[...], w_ref[...], NT)
    grad_ref[...] = grad
    y, r, v, gate = mixed_ref[...], r_ref[...], v_ref[...], gate_ref[...]
    unit, scale = group_norm(y)
    rate = jax.nn.sigmoid(rp_ref[...])
    mod = k_ref[...] * (1.0 + (rate - 1.0) * vec[1:2])
    dot_sum = head_sum(r * mod * vec[2:3])
    q = grad * gate
    dunit = q * vec[3:4]
    dy = scale * (
        dunit - head_sum(dunit) * (1.0 / HEAD) - unit * (head_sum(dunit * unit) * (1.0 / HEAD))
    )
    dy_ref[...] = dy
    full = mm(reach_ref[...], dy, TN)
    state_ref[0] = squeeze(jnp.where(same_head(PAIR, HEAD), full, 0.0)).astype(BF)
    dgate_ref[...] = grad * (unit * vec[3:4] + vec[4:5] + dot_sum * v)
    dsum = head_sum(q * v)
    ds_ref[...] = dsum
    row = lambda x: jnp.sum(x, 0, keepdims=True)
    zero = jnp.zeros((5, PAIR), FL)
    sums_ref[...] = jnp.concatenate([row(dsum * r * mod), row(q * unit), row(q), zero], 0)


def head_back(middle, w, mixed, reach, r, k, v, rp, gate, vec):
    count, local = r.shape
    width = w.shape[1]
    pairs = local // PAIR
    return pl.pallas_call(
        head_back_kernel,
        grid=(pairs,),
        in_specs=[full(middle.shape), pl.BlockSpec((PAIR, width), lambda p: (p, 0))]
        + [pair_spec(count)] * 7
        + [pair_spec(8)],
        out_specs=[pair_spec(count)] * 4 + [pair_spec(8), block_spec(HEAD, PAIR)],
        out_shape=[jax.ShapeDtypeStruct((count, local), FL)] * 4
        + [
            jax.ShapeDtypeStruct((8, local), FL),
            jax.ShapeDtypeStruct((pairs, HEAD, PAIR), BF),
        ],
        name="head_back",
    )(middle, w, mixed, reach, r, k, v, rp, gate, vec)


def leave_kernel(s_ref, *refs):
    half = (len(refs) - 1) // 2
    moves, adds, out_ref = refs[:half], refs[half:-1], refs[-1]
    place = s_ref[4]
    size = half + 1
    for p in range(out_ref.shape[0]):
        state = jnp.zeros((PAIR, PAIR), FL)
        for ahead in range(half, 0, -1):
            slot = size - ahead - 1
            move = spread(moves[slot][p, 0].astype(FL)).astype(BF)
            high, low = parts(state)
            new = dot(move, high, TN) + dot(move, low, TN) + spread(adds[slot][p].astype(FL))
            state = jnp.where(place + ahead < size, new, 0.0)
        out_ref[p] = squeeze(state)


def leave_grad(scalars, moves, adds):
    pairs = adds[0].shape[0]
    return pl.pallas_call(
        leave_kernel,
        in_specs=[pl.BlockSpec(memory_space=pltpu.SMEM)] + whole(len(moves) + len(adds)),
        out_specs=whole(1)[0],
        out_shape=jax.ShapeDtypeStruct((pairs, HEAD, PAIR), FL),
        name="leave_grad",
    )(scalars, *moves, *adds)


def scan_back_kernel(
    grad_ref, dy_ref, ds_ref, r_ref, k_ref, v_ref, dp_ref, rp_ref, gate_ref, vec_ref,
    inverse_ref, enter_ref, leave_ref,
    dr_ref, dk_ref, dv_ref, ddp_ref, drp_ref, sums_ref,
):
    vec = vec_ref[...]
    r, k, v = r_ref[...], k_ref[...], v_ref[...]
    count = r.shape[0]
    span = span_of(count)
    chunks = count // span
    sig, logd, rate, inv_norm, unit, mod, removal = prepare(k, dp_ref[...], rp_ref[...], vec)
    dsum = ds_ref[...]
    state = spread(enter_ref[0])
    kept = []
    for index in range(chunks):
        at = slice(index * span, (index + 1) * span)
        q = chunk_of(r[at], v[at], logd[at], unit[at], mod[at], removal[at])
        inverse = parts(spread(inverse_ref[0, index]))
        vs, hs = parts(q["v"]), parts(state)
        along = mm(inverse, mm(q["ue"], hs) + mm(q["uk"], vs))
        kept.append((at, q, inverse, vs, state, hs, along))
        if index + 1 < chunks:
            end = jnp.sum(diagonal(q["end"]), 1, keepdims=True)
            state = end * state + mm(q["kd"], vs, TN) - mm(q["bd"], along, TN)
    leave = spread(leave_ref[0])
    tails = []
    for at, q, inverse, vs, state, hs, along in reversed(kept):
        dy = parts(spread(dy_ref[at, :]))
        lp = parts(leave)
        along_p = parts(along)
        kd, bd = parts(q["kd"]), parts(q["bd"])
        dalong = -(mm(q["rb"], dy, TN) + mm(bd, lp))
        z = mm(inverse, dalong, TN)
        zp = parts(z)
        dv = mm(q["rk"], dy, TN) + mm(kd, lp) + mm(q["uk"], zp, TN)
        end = jnp.sum(diagonal(q["end"]), 1, keepdims=True)
        ue, re, kl, bl = parts(q["ue"]), parts(q["re"]), parts(q["kl"]), parts(q["bl"])
        dstate = end * leave + mm(re, dy, TN) + mm(ue, zp, TN)
        rk = parts(jnp.where(q["inclusive"], mm(dy, vs, NT), 0.0))
        rb = parts(jnp.where(q["inclusive"], -mm(dy, along_p, NT), 0.0))
        uk = parts(jnp.where(q["strict"], mm(zp, vs, NT), 0.0))
        ub = parts(jnp.where(q["strict"], -mm(zp, along_p, NT), 0.0))
        dre = mm(dy, hs, NT) + mm(rk, kl) + mm(rb, bl)
        due = mm(zp, hs, NT) + mm(uk, kl) + mm(ub, bl)
        dkl = mm(rk, re, TN) + mm(uk, ue, TN)
        dbl = mm(rb, re, TN) + mm(ub, ue, TN)
        dkd = mm(vs, lp, NT)
        dbd = -mm(along_p, lp, NT)
        inside = squeeze(dre * q["re"] - dkl * q["kl"] - dbl * q["bl"] - dkd * q["kd"] - dbd * q["bd"])
        early = squeeze(due * q["ue"])
        ends = jnp.sum(squeeze(dkd * q["kd"] + dbd * q["bd"]), 0, keepdims=True)
        ones = jnp.ones((8, PAIR), BF)
        ends = ends + mm_ones(ones, state * leave, NT)[0:1] * q["end"]
        dlog = (
            mm_ones(tri(span, False, True).astype(FL).astype(BF), inside)
            + mm_ones(tri(span, True, True).astype(FL).astype(BF), early)
            + ends
        )
        dr = squeeze(dre) * q["c"]
        dunit = squeeze(due) * q["before"]
        dmod = squeeze(dkl) * q["inverse"] + squeeze(dkd) * q["ratio"]
        dremoval = squeeze(dbl) * q["inverse"] + squeeze(dbd) * q["ratio"]
        leave = dstate
        r_, k_, rate_, mod_, unit_ = r[at], k[at], rate[at], mod[at], unit[at]
        bonus = dsum[at] * vec[2:3]
        dot_sum = head_sum(r_ * mod_ * vec[2:3])
        dr_ref[at, :] = (dr + bonus * mod_).astype(BF)
        dv_ref[at, :] = (squeeze(dv) + grad_ref[at, :] * gate_ref[at, :] * dot_sum).astype(BF)
        dmod = dmod + bonus * r_
        drate = dremoval * unit_ + dmod * k_ * vec[1:2]
        dunit = dunit + dremoval * rate_
        dscaled = inv_norm[at] * (dunit - unit_ * head_sum(dunit * unit_))
        dk_ref[at, :] = (dmod * (1.0 + (rate_ - 1.0) * vec[1:2]) + dscaled * vec[0:1]).astype(BF)
        drp = drate * rate_ * (1.0 - rate_)
        ddp = dlog * (-DECAY_SCALE) * sig[at] * (1.0 - sig[at])
        drp_ref[at, :] = drp.astype(BF)
        ddp_ref[at, :] = ddp.astype(BF)
        row = lambda x: jnp.sum(x, 0, keepdims=True)
        tails.append(
            jnp.concatenate(
                [row(ddp), row(drp), row(dscaled * k_), row(dmod * k_ * (rate_ - 1.0)), jnp.zeros((4, PAIR), FL)],
                0,
            )
        )
    sums_ref[...] = sum(tails[1:], tails[0])


def scan_back(grad, dy, ds, r, k, v, dp, rp, gate, vec, inverse, enter, leave):
    count, local = r.shape
    pairs = local // PAIR
    span = span_of(count)
    chunks = count // span
    return pl.pallas_call(
        scan_back_kernel,
        grid=(pairs,),
        in_specs=[pair_spec(count)] * 9
        + [
            pair_spec(8),
            block_spec(chunks, span, 2 * span),
            block_spec(HEAD, PAIR),
            block_spec(HEAD, PAIR),
        ],
        out_specs=[pair_spec(count)] * 5 + [pair_spec(8)],
        out_shape=[jax.ShapeDtypeStruct((count, local), BF)] * 5
        + [jax.ShapeDtypeStruct((8, local), FL)],
        name="scan_back",
    )(grad, dy, ds, r, k, v, dp, rp, gate, vec, inverse, enter, leave)


def block(inputs, cotangent, vectors, mix_w, out_w, down_w, up_w, key_w, value_w):
    seq, tp = lax.axis_size("seq"), lax.axis_size("tp")
    count = seq // 2
    place, t = lax.axis_index("seq"), lax.axis_index("tp")
    i, j = place // 2, place % 2
    rows, width = inputs.shape
    tokens = cotangent.shape[0]
    local = mix_w.shape[2]
    part = width // seq
    rank = down_w.shape[1]
    quarter = rank // tp
    total = seq * tp
    scalars = jnp.stack([i, j, t, jnp.where(place + t == 0, 1, 0), place]).astype(jnp.int32)

    def swap(x):
        return lax.ppermute(x, "seq", [(s, s ^ 1) for s in range(seq)])

    def shift(x, k):
        route = [(2 * a + b, 2 * ((a + k) % count) + b) for a in range(count) for b in range(2)]
        return lax.ppermute(x, "seq", route)

    def turn(x, k):
        return lax.ppermute(x, "seq", [(s, (s + k) % seq) for s in range(seq)])

    def shift_t(x, k):
        return lax.ppermute(x, "tp", [(a, (a + k) % tp) for a in range(tp)])

    def next_rows(x, step):
        route = [(d, d + step) for d in range(total) if 0 <= d + step < total]
        return lax.ppermute(x, ("seq", "tp"), route)

    def to_columns(slots):
        return [slots[0]] + [shift(slots[k], k) for k in range(1, count)]

    def to_pieces(slots):
        return [shift(x, -(k + 1)) for k, x in enumerate(slots)]

    def to_owners(sent):
        return [shift_t(x, m + 1) for m, x in enumerate(sent)]

    def gather_i(x):
        return [x] + [shift(x, k) for k in range(1, count)]

    def join(slots):
        (out,) = run(
            join_kernel, scalars, slots, [shaped(count, *slots[0].shape, dtype=slots[0].dtype)]
        )
        return out

    def spread_rows(kernel, ins, c):
        slots = run(
            kernel,
            scalars,
            ins,
            [shaped(c, 2, rows, part, dtype=BF)] * count,
            [pltpu.VMEM((count, c, 2, rows, part), BF)],
        )
        slots = to_columns(slots)
        return lax.all_gather(join(slots), "tp")

    def collect(own, sent):
        got = to_owners(sent)
        c = own.shape[0]
        slots = run(collect_kernel, scalars, (own, *got), [shaped(c, 2, rows, part)] * count)
        return [slots[0]] + to_pieces(slots[1:])

    store = pltpu.VMEM((count, 2, 1, rows, part), FL)
    store_two = pltpu.VMEM((count, 2, 2, rows, part), FL)

    before_rows = next_rows(inputs[-1:], 1)
    mix_n = swap(mix_w)
    down_o = lax.all_gather(down_w, "tp", axis=0, tiled=True)
    down_n = swap(down_o)
    up_n = swap(up_w)
    up_pair = jnp.where(j == 0, jnp.concatenate([up_w, up_n], 0), jnp.concatenate([up_n, up_w], 0))
    up_slots = jnp.stack(gather_i(up_pair)[::-1])
    up = lax.dynamic_slice_in_dim(
        jnp.concatenate([up_slots, up_slots], 0), count - 1 - i, count, 0
    ).reshape(rank, local)
    value_n = swap(value_w)
    key_n = swap(key_w)
    full_out = lax.all_gather(out_w, "seq", axis=1, tiled=True)
    columns = lax.dynamic_slice_in_dim(vectors, t * local, local, 1)
    kernel_vec = jnp.concatenate([columns[12:17], jnp.zeros((3, local), FL)], 0)
    block_vec = lax.dynamic_index_in_dim(
        vectors[4:10].reshape(6, count, 2, part).transpose(1, 2, 0, 3), i, 0, False
    )
    block_vec = jnp.where(j == 0, block_vec, block_vec[::-1])
    block_vec = jnp.concatenate([block_vec, jnp.zeros((2, 2, part), FL)], 1)

    g_one = spread_rows(rows_in_kernel, (inputs, before_rows, vectors), 2)
    wide = 3 * local + quarter
    own, *sent = run(
        mix_forward_kernel,
        scalars,
        (g_one, block_vec, mix_w, mix_n, down_o, down_n),
        [shaped(tokens, wide)] + [shaped(tokens + 16, wide, dtype=BF)] * (count - 1),
        [pltpu.VMEM((tokens, rank), FL)],
    )
    got = to_pieces(sent)
    low = total_of(own[:, 3 * local :], [x[:, 3 * local :] for x in got])
    low = lax.all_gather(low, "tp")
    accept, keys, values, decay_pre, rate_pre, gate, reach, local_out, state, inverse = local_scan(
        low, up, columns[10:12], kernel_vec, own, got
    )
    states = [turn(state, k) for k in range(1, seq)]
    mixer, mixed, enter, own, *sent = finish_forward(
        scalars, states, tp, reach, local_out, accept, keys, values, rate_pre, gate, kernel_vec, full_out
    )
    got = to_owners(sent)
    middle, normed2, last2 = run(
        rows_mid_kernel,
        scalars,
        (inputs, vectors, own, *got),
        [shaped(rows, width), shaped(rows, width, dtype=BF), shaped(1, width, dtype=BF)],
    )
    edge2 = next_rows(last2, 1)

    cots = run(
        split_kernel,
        scalars,
        (cotangent,),
        [shaped(1, 2, tokens, part, dtype=BF)] * count,
        [pltpu.VMEM((count, 1, 2, tokens, part), BF)],
    )
    cots = to_columns(cots)
    own, *sent = value_back(cots, value_w, value_n)
    grad_hidden = own
    for x in to_pieces(sent):
        grad_hidden = grad_hidden + x.astype(FL)
    g_two = spread_rows(rows_ffn_kernel, (normed2, edge2, vectors), 1)
    own, *sent = key_forward(g_two, key_w, key_n)
    active = own
    for x in to_pieces(sent):
        active = active + x.astype(FL)
    active = jax.nn.relu(active)
    grad_pre = gather_i((grad_hidden * 2.0 * active).astype(BF))
    hidden = gather_i((active * active).astype(BF))
    own, *sent = ffn_back(scalars, grad_pre, key_w, key_n, True, tp)
    grad_ffn, spill2 = run(
        rows_back_kernel,
        scalars,
        (vectors, *collect(own, sent)),
        [shaped(rows, width), shaped(1, width)],
        [store],
    )
    next2 = next_rows(spill2, -1)
    grad_middle, middle_low, sums_two = run(
        middle_back_kernel,
        scalars,
        (grad_ffn, next2, middle, normed2, edge2, cotangent, vectors),
        [shaped(rows, width), shaped(rows, width, dtype=BF), shaped(3, width)],
    )
    middle_grad = lax.all_gather(middle_low, "tp", axis=0, tiled=True)

    grad_mixer, dy, dgate, dsum, sums_a, state_grad = head_back(
        middle_grad, full_out, mixed, reach, accept, keys, values, rate_pre, gate, kernel_vec
    )
    state_grads = [turn(state_grad, k) for k in range(1, seq)]
    leave = leave_grad(scalars, states, state_grads)
    d_accept, d_keys, d_values, d_decay, d_rate, sums_b = scan_back(
        grad_mixer, dy, dsum, accept, keys, values, decay_pre, rate_pre, gate, kernel_vec,
        inverse, enter, leave,
    )
    own, *sent, up_part = run(
        lora_back_kernel,
        scalars,
        (low, up, d_decay, d_rate, dgate),
        [shaped(tokens, quarter)]
        + [shaped(tokens, quarter, dtype=BF)] * (tp - 1)
        + [shaped(rank, local, dtype=BF)],
        [pltpu.VMEM((tokens, rank), FL)],
    )
    inner = own
    for x in to_owners(sent):
        inner = inner + x.astype(FL)
    inner = gather_i(inner.astype(BF))
    inner = lax.all_gather(join(inner), "tp")
    grads = [x for g in (d_accept, d_keys, d_values) for x in gather_i(g)]
    shape = (2, count, 2, rows, part)
    own, *sent, mu_part = run(
        functools.partial(mix_back_kernel, count),
        scalars,
        (g_one, block_vec, inner, *grads, mix_w, mix_n, down_o, down_n),
        [shaped(*shape)] + [shaped(*shape, dtype=BF)] * (tp - 1) + [shaped(2, 8, part)],
        [pltpu.VMEM((2, count, 2, tokens, part), FL)],
    )
    staying, carried, spill1 = run(
        rows_two_kernel,
        scalars,
        collect(own, sent),
        [shaped(rows, width), shaped(rows, width), shaped(1, width)],
        [store_two],
    )
    next1 = next_rows(spill1, -1)
    grad_inputs, sums_one = run(
        first_back_kernel,
        scalars,
        (inputs, staying, carried, next1, grad_middle, vectors),
        [shaped(rows, width), shaped(2, width)],
    )

    own, *sent = ffn_back(scalars, hidden, value_w, value_n, False, tp)
    (output,) = run(
        output_kernel,
        scalars,
        (middle, *collect(own, sent)),
        [shaped(rows, width, dtype=BF)],
        [store],
    )

    def joined(pair):
        return pair[0] + swap(pair[1]).astype(FL)

    grad_value = joined(value_grad(hidden, cots))
    grad_key = joined(key_grad(g_two, grad_pre))
    grad_out = lax.psum_scatter(
        dot(mixer, middle_grad, TN).astype(BF), "seq", scatter_dimension=1, tiled=True
    ).astype(FL)
    grad_up = lax.psum_scatter(up_part, "seq", scatter_dimension=0, tiled=True).astype(FL)
    shape = (3, part, local)
    mix_o, mix_s, down_go, down_gn = run(
        functools.partial(mix_grad_kernel, count),
        scalars,
        (g_one, block_vec, inner, *grads),
        [shaped(*shape), shaped(*shape, dtype=BF), shaped(part, rank), shaped(part, rank, dtype=BF)],
    )
    grad_mix = joined((mix_o, mix_s))
    share = part // tp
    grad_down = joined(
        [lax.dynamic_slice_in_dim(x, t * share, share, 0) for x in (down_go, down_gn)]
    )
    mu_rows = jnp.where(j == 0, mu_part, mu_part[::-1])[:, :6].transpose(1, 0, 2).reshape(6, 2 * part)
    placed_mu = lax.dynamic_update_slice_in_dim(
        jnp.zeros((6, width), FL), mu_rows, i * 2 * part, 1
    )
    placed = lax.dynamic_update_slice_in_dim(
        jnp.zeros((7, width), FL), jnp.concatenate([sums_b[:4], sums_a[:3]], 0), t * local, 1
    )
    grad_vec = jnp.concatenate([sums_one, sums_two[:2], placed_mu, placed, sums_two[2:]], 0)
    grad_vec = grad_vec.reshape(18, total, width // total).transpose(1, 0, 2)
    grad_vec = jnp.sum(lax.all_to_all(grad_vec, ("seq", "tp"), 0, 0, tiled=True), 0)
    return (
        output,
        grad_inputs,
        grad_vec,
        grad_mix,
        grad_out,
        grad_down,
        grad_up,
        grad_key,
        grad_value,
    )


def solution(mesh):
    placed = (
        P(("seq", "tp"), None),
        P("seq", None),
        P(),
        P(None, "seq", "tp"),
        P("tp", "seq"),
        P(("seq", "tp"), None),
        P("seq", "tp"),
        P("seq", "tp"),
        P("tp", "seq"),
    )
    return jax.shard_map(
        block,
        mesh=mesh,
        in_specs=placed,
        out_specs=(
            P(("seq", "tp"), None),
            P(("seq", "tp"), None),
            P(None, ("seq", "tp")),
            P(None, "seq", "tp"),
            P("tp", "seq"),
            P(("seq", "tp"), None),
            P("seq", "tp"),
            P("seq", "tp"),
            P("tp", "seq"),
        ),
        check_vma=False,
    )
```
